32 devices in a mesh: videos: 2 (over y), tm: 8 (over z, x), tile: 2 (over core).
Axes of the slice: x: 2, y: 2, z: 4, core: 2. Of those that a mesh axis runs over, the one named last changes fastest.
Arguments:
- latents: bfloat16 [32, 8, 32, 384], P(('videos', 'tm'), None, 'tile'), parts along dimension 0, may hold values from -6 to 6, as said below
- frame_counts: int32 [16], P(('videos', 'tm')), parts along dimension 0, may hold values from 1 to 2, as said below
- owners: int32 [32], P('videos'), parts along dimension 0, may hold values from 0 to 1
- w_time: bfloat16 [3, 384, 768], replicated, may hold values from -0.1875 to 0.1875
- b_time: float32 [768], replicated, may hold values from -3 to 3
- w_up: bfloat16 [3, 3, 384, 192], replicated, may hold values from -0.109375 to 0.109375
- b_up: float32 [192], replicated, may hold values from -3 to 3
Outputs:
- decoded: bfloat16 [64, 16, 12288], P(('videos', 'tm'), None, 'tile'), parts along dimension 0
The draws below stay inside these ranges and needn't reach their ends.
There are 2 independent parts, one for each index of `videos`. The reference program is written for one: setup_inputs(seed, part) draws one part's arguments, and reference() takes and returns one part's arrays. A program takes and returns all parts, laid end to end along the dimension named above; an argument that names none is the same for every part. Nothing has to cross between parts.
Inputs may be any that keep to these rules, and one draw needn't show every extreme that they name: `frame_counts`: every device has one or two valid frames; in every draw some device has two and some has one. `latents`: in every slot and row, stored columns 12 to 15 of tile 0 equal the first 4 stored columns of tile 1.
All inputs are finite; a program needn't handle non-finite values.
Results may differ from the reference program's by a relative error of at most 0.0047.
Values may be sent and summed in bfloat16 or wider, within the bound.
No kernel may reach another device: no remote copies, remote signals or barrier semaphores. Data moves between devices by JAX's collectives and lax.ppermute only.
A program may use at most 128 MiB of HBM per device.

```python
import jax
import jax.numpy as jnp
from jax import lax

C = 384
CO = 192
SLOTS = 2
HT = 8
WT = 16
OV = 4
FR = 16
N_TM = 8


def draw_frame_counts(key, part):
    counts = jax.random.randint(key, (N_TM,), 1, 3)
    first = jax.random.randint(jax.random.fold_in(key, 7), (), 0, N_TM)
    second = (first + 1 + jax.random.randint(jax.random.fold_in(key, 8), (), 0, N_TM - 1)) % N_TM
    counts = counts.at[first].set(2).at[second].set(1)
    return counts.astype(jnp.int32)


def draw_latents(key, part):
    shape = (FR, HT, 2 * WT - OV, C)
    image = jnp.clip(jax.random.normal(key, shape, jnp.float32), -6.0, 6.0)
    tiles = jnp.concatenate([image[:, :, 0:WT, :], image[:, :, WT - OV:, :]], 2)
    return tiles.astype(jnp.bfloat16)


def touch_ends(array, rng, smallest, high):
    longest = array.shape.index(max(array.shape))
    spots = []
    for shift in (0, 1):
        where = [jax.random.randint(jax.random.fold_in(rng, axis), (), 0, length) for axis, length in enumerate(array.shape)]
        where[longest] = (where[longest] + shift) % array.shape[longest]
        spots.append(tuple(where))
    return array.at[spots[0]].set(smallest).at[spots[1]].set(high)


def centred(stream_key, dims, width, bound, kind=jnp.bfloat16):
    return jnp.clip(width * jax.random.normal(stream_key, dims, jnp.float32), -bound, bound).astype(kind)


def setup_inputs(seed: int = 0, part: int = 0) -> dict:
    keys = jax.random.split(jax.random.key(seed), 8)
    part_splits = jax.random.split(jax.random.fold_in(keys[7], part), 8)
    latents = draw_latents(jax.random.fold_in(jax.random.fold_in(keys[7], part), 71), part)
    frame_counts = draw_frame_counts(jax.random.fold_in(jax.random.fold_in(keys[7], part), 71), part)
    owners = touch_ends(jax.random.randint(part_splits[2], (2 * HT,), 0, 2), jax.random.fold_in(part_splits[2], 1), 0, 1).astype(jnp.int32)
    w_time = centred(keys[3], (3, C, 2 * C), (3 * C) ** -0.5, 0.1875)
    b_time = centred(keys[4], (2 * C,), 0.5, 3.0, jnp.float32)
    w_up = centred(keys[5], (3, 3, C, CO), (9 * C) ** -0.5, 0.109375)
    b_up = centred(keys[6], (CO,), 0.5, 3.0, jnp.float32)
    return dict(latents=latents, frame_counts=frame_counts, owners=owners, w_time=w_time, b_time=b_time, w_up=w_up, b_up=b_up)


def to_frames(tconv):
    count, rows, cols, both = tconv.shape
    half = both // 2
    return tconv.reshape(count, rows, cols, 2, half).transpose(0, 3, 1, 2, 4).reshape(2 * count, rows, cols, half)


def upconv(frames, w_up, b_up):
    count, rows, cols, chans = frames.shape
    big = jnp.repeat(jnp.repeat(frames, 2, axis=1), 2, axis=2)
    padded = jnp.pad(big, ((0, 0), (1, 1), (1, 1), (0, 0)))
    outc = w_up.shape[3]
    total = jnp.zeros((count * 4 * rows * cols, outc), jnp.float32)
    for row_tap in range(3):
        pieces = jnp.concatenate([padded[:, row_tap:row_tap + 2 * rows, col_tap:col_tap + 2 * cols, :] for col_tap in range(3)], -1)
        total = total + jnp.dot(pieces.reshape(-1, 3 * chans), w_up[row_tap].reshape(3 * chans, outc), preferred_element_type=jnp.float32)
    total = total + b_up
    return total.reshape(count, 2 * rows, 2 * cols, outc).astype(jnp.bfloat16)


def reference(latents, frame_counts, owners, w_time, b_time, w_up, b_up):
    slot_ids = jnp.arange(FR, dtype=jnp.int32)
    device = slot_ids // SLOTS
    within = slot_ids % SLOTS
    starts = jnp.cumsum(frame_counts) - frame_counts
    position = (starts[device] + within).astype(jnp.int32)
    valid = within < frame_counts[device]
    target = jnp.where(valid, position, FR).astype(jnp.int32)
    packed = jnp.zeros_like(latents).at[target].set(latents, mode="drop")
    ext = jnp.concatenate([jnp.zeros((2,) + latents.shape[1:], latents.dtype), packed], 0)
    stacked = jnp.concatenate([ext[0:FR], ext[1:FR + 1], ext[2:FR + 2]], -1)
    tconv = jnp.dot(stacked.reshape(-1, 3 * C), w_time.reshape(3 * C, 2 * C), preferred_element_type=jnp.float32) + b_time
    tconv = tconv.reshape(FR, HT, 2 * WT, 2 * C).astype(jnp.bfloat16)
    tconv = tconv[jnp.minimum(position, FR - 1).astype(jnp.int32)]
    frames = to_frames(tconv)

    def decode_tile(first):
        def one_slot(pair):
            return upconv(pair, w_up, b_up)
        tile_frames = lax.dynamic_slice_in_dim(frames, first, WT, 2).reshape(FR, 2, HT, WT, C)
        return lax.map(one_slot, tile_frames).reshape(2 * FR, 2 * HT, 2 * WT, CO)

    left = decode_tile(0).astype(jnp.float32)
    right = decode_tile(WT).astype(jnp.float32)
    strip = 2 * OV
    weight = (strip - jnp.arange(strip, dtype=jnp.float32) - 0.5) / strip
    blend = left[:, :, 2 * WT - strip:, :] * weight[:, None] + right[:, :, :strip, :] * (1.0 - weight[:, None])
    keep_left = (owners == 0)[None, :, None, None]
    keep_right = (owners == 1)[None, :, None, None]
    left = left.at[:, :, 2 * WT - strip:, :].set(jnp.where(keep_left, blend, 0.0))
    right = right.at[:, :, :strip, :].set(jnp.where(keep_right, blend, 0.0))
    whole = jnp.concatenate([left, right], 2)
    frame_valid = jnp.repeat(valid, 2)[:, None, None, None]
    whole = jnp.where(frame_valid, whole, 0.0)
    return whole.reshape(2 * FR, 2 * HT, 2 * 2 * WT * CO).astype(jnp.bfloat16)
```

```python
import functools

import jax
import jax.numpy as jnp
from jax import lax
from jax.experimental import pallas as pl
from jax.experimental.pallas import tpu as pltpu
from jax.sharding import PartitionSpec as P

OV = 4
F32 = jnp.float32
BF16 = jnp.bfloat16


def dot(a, b):
    return jnp.dot(a, b, preferred_element_type=F32)


def prepare_weights(w_up, wc, wl, wr):
    chans, outc = w_up.shape[2], w_up.shape[3]
    blank = jnp.zeros((chans, 64), F32)
    for pr, block, rows in ((0, 0, (0,)), (0, 1, (1, 2)), (1, 0, (0, 1)), (1, 1, (2,))):
        taps = []
        for col in range(3):
            tap = w_up[rows[0], col].astype(F32)
            for row in rows[1:]:
                tap = tap + w_up[row, col].astype(F32)
            taps.append(tap)
        span = pl.ds(block * chans, chans)
        wc[pr, span, :] = jnp.concatenate([taps[1] + taps[2], taps[0] + taps[1]], -1).astype(BF16)
        wl[pr, span, :] = jnp.concatenate([taps[0], blank], -1).astype(BF16)
        wr[pr, span, :] = jnp.concatenate([blank, taps[2]], -1).astype(BF16)


def placement(rows, cols):
    height, depth = 3 * cols * 2 * rows, 2 * rows * cols
    i = lax.broadcasted_iota(jnp.int32, (height, depth), 0)
    k = lax.broadcasted_iota(jnp.int32, (height, depth), 1)
    group = cols * 2 * rows
    shift = i // group
    col = (i % group) // (2 * rows)
    half = (i % (2 * rows)) // rows
    row = i % rows + shift - 1
    hit = (k == half * rows * cols + row * cols + col) & (row >= 0) & (row < rows)
    return jnp.where(hit, 1.0, 0.0).astype(BF16)


def picker(rows, cols, col):
    i = lax.broadcasted_iota(jnp.int32, (2 * rows, rows * cols), 0)
    k = lax.broadcasted_iota(jnp.int32, (2 * rows, rows * cols), 1)
    return jnp.where((i < rows) & (k == i * cols + col), 1.0, 0.0).astype(BF16)


def row_shifts(t):
    row = lax.broadcasted_iota(jnp.int32, t.shape, 0)
    up = jnp.where(row == 0, 0.0, pltpu.roll(t, 1, 0))
    down = jnp.where(row == t.shape[0] - 1, 0.0, pltpu.roll(t, t.shape[0] - 1, 0))
    return up, t, down


def fill_x(t, mine, place, x, rows, cols):
    chans = t.shape[1] // 2
    pixels = rows * cols
    body = t[:pixels].astype(BF16)
    both = jnp.concatenate([body[:, :chans], body[:, chans:]], 0)
    spread = dot(place, both).astype(BF16)
    height = 2 * pixels
    edge = t[pixels : pixels + rows].astype(BF16).astype(F32)
    for v, shifted in enumerate(row_shifts(edge)):
        lanes = pl.ds(v * chans, chans)
        x[pl.ds(2 * rows, height), lanes] = spread[v * height : (v + 1) * height]
        column = jnp.concatenate([shifted[:, :chans], shifted[:, chans:]], 0)
        x[pl.ds(0, 2 * rows), lanes] = jnp.where(mine == 1, column, 0.0).astype(BF16)
        x[pl.ds(2 * rows + height, 2 * rows), lanes] = jnp.where(mine == 0, column, 0.0).astype(BF16)


def convolve(x, wc, wl, wr, bias, owners, mine, valid, wide, out, first, rows, cols):
    chans2 = wc.shape[1]
    chans = chans2 // 2
    height = 2 * rows * cols
    lanes = wc.shape[2]
    part = wl.shape[2]
    col_of = lax.broadcasted_iota(jnp.int32, (height, 1), 0) // (2 * rows)
    strip_from = jnp.where(mine == 0, cols - OV, 0)
    soft = 1.0 - 0.5 / (2 * OV)
    scale_l = jnp.where(col_of == strip_from, soft, 1.0)
    scale_r = jnp.where(col_of == strip_from + OV - 1, soft, 1.0)
    for pr in range(2):
        span = pl.ds(pr * chans, chans2)
        mid = dot(x[pl.ds(2 * rows, height), span], wc[pr])
        left = dot(x[pl.ds(0, height), span], wl[pr]) * scale_l
        right = dot(x[pl.ds(4 * rows, height), span], wr[pr]) * scale_r
        low = mid[:, : lanes - part] + left[:, : lanes - part]
        centre = mid[:, lanes - part : part] + left[:, lanes - part :] + right[:, : 2 * part - lanes]
        high = mid[:, part:] + right[:, 2 * part - lanes :]
        y = jnp.concatenate([low, centre, high], -1) + bias
        for col in range(cols):
            for h in range(2):
                top = col * 2 * rows + h * rows
                for j in range(lanes // 128):
                    wide[h, col * lanes // 128 + j, pl.ds(pr, rows, stride=2), :] = y[
                        top : top + rows, j * 128 : (j + 1) * 128
                    ]
    out_row = lax.broadcasted_iota(jnp.int32, (2 * rows, 128), 0)
    keep = jnp.zeros((2 * rows, 128), jnp.int32)
    for r in range(2 * rows):
        keep = jnp.where(out_row == r, owners[r], keep)
    keep = jnp.where(keep == mine, 1.0, 0.0)
    shown = jnp.where(valid, 1.0, 0.0)
    for col in range(cols):
        in_strip = (col >= strip_from) & (col < strip_from + OV)
        mask = jnp.where(in_strip, keep, 1.0) > 0.5
        for h in range(2):
            for lane in range(col * lanes, (col + 1) * lanes, 128):
                block = wide[h, lane // 128]
                block = jnp.where(mask & (shown > 0.5), block, 0.0)
                out[first + h, :, pl.ds(lane, 128)] = block.astype(BF16)


def kernel(
    facts, owners, own, own_far, near, near_far, far, far_far, w_time, b_time, w_up, b_up,
    out, lhs, x, wc, wl, wr, wide,
):
    slots, rows, cols, chans = own.shape
    pixels = rows * cols
    mine, count, count_near, place_tm = facts[0], facts[1], facts[2], facts[3]
    prepare_weights(w_up, wc, wl, wr)
    pick = picker(rows, cols, jnp.where(mine == 0, OV, cols - OV - 1))

    def fill(k, main, other, on):
        main = jnp.where(on, main, jnp.zeros_like(main))
        other = jnp.where(on, other, jnp.zeros_like(other))
        lhs[k, pl.ds(0, pixels), :] = main
        lhs[k, pl.ds(pixels, 2 * rows), :] = dot(pick, other).astype(BF16)

    flat = lambda v: v.reshape(pixels, chans)
    near_two = count_near == 2
    older = jnp.where(near_two, flat(near[0]), flat(far[0]))
    older_far = jnp.where(near_two, flat(near_far[0]), flat(far_far[0]))
    newer = jnp.where(near_two, flat(near[1]), flat(near[0]))
    newer_far = jnp.where(near_two, flat(near_far[1]), flat(near_far[0]))
    fill(0, older, older_far, (place_tm >= 2) | ((place_tm == 1) & near_two))
    fill(1, newer, newer_far, place_tm >= 1)
    fill(2, flat(own[0]), flat(own_far[0]), place_tm >= 0)
    fill(3, flat(own[1]), flat(own_far[1]), place_tm >= 0)
    place = placement(rows, cols)
    bias = jnp.concatenate([b_up[...], b_up[...]], -1)
    for slot in range(2):
        t = b_time[...] + dot(lhs[slot], w_time[0])
        t = t + dot(lhs[slot + 1], w_time[1])
        t = t + dot(lhs[slot + 2], w_time[2])
        fill_x(t, mine, place, x, rows, cols)
        convolve(x, wc, wl, wr, bias, owners, mine, slot < count, wide, out, 2 * slot, rows, cols)


def per_device(latents, frame_counts, owners, w_time, b_time, w_up, b_up):
    slots, rows, cols, chans = latents.shape
    outc = w_up.shape[3]
    ring = lax.axis_size("tm")
    place_tm = lax.axis_index("tm")
    mine = lax.axis_index("tile")
    count = frame_counts[0]
    other = [(0, 1), (1, 0)]
    step = lambda k: [(i, (i + k) % ring) for i in range(ring)]
    near = lax.ppermute(latents, "tm", step(1))
    latest = lax.dynamic_slice_in_dim(latents, count - 1, 1, 0)
    far = lax.ppermute(latest, "tm", step(2))
    count_near = lax.ppermute(frame_counts, "tm", step(1))
    own_far = lax.ppermute(latents, "tile", other)
    near_far = lax.ppermute(near, "tile", other)
    far_far = lax.ppermute(far, "tile", other)
    facts = jnp.stack([mine, count, count_near[0], place_tm]).astype(jnp.int32)
    smem = pl.BlockSpec(memory_space=pltpu.SMEM)
    vmem = pl.BlockSpec(memory_space=pltpu.VMEM)
    wide_lanes = 2 * cols * outc
    return pl.pallas_call(
        kernel,
        out_shape=jax.ShapeDtypeStruct((2 * slots, 2 * rows, wide_lanes), BF16),
        in_specs=[smem, smem] + [vmem] * 10,
        out_specs=vmem,
        scratch_shapes=[
            pltpu.VMEM((4, rows * cols + 2 * rows, chans), BF16),
            pltpu.VMEM(((cols + 2) * 2 * rows, 3 * chans), BF16),
            pltpu.VMEM((2, 2 * chans, 2 * outc), BF16),
            pltpu.VMEM((2, 2 * chans, 256), BF16),
            pltpu.VMEM((2, 2 * chans, 256), BF16),
            pltpu.VMEM((2, wide_lanes // 128, 2 * rows, 128), F32),
        ],
        compiler_params=pltpu.CompilerParams(vmem_limit_bytes=40 << 20),
        cost_estimate=pl.CostEstimate(flops=2 * 10**9, bytes_accessed=4 << 20, transcendentals=0),
    )(
        facts, owners, latents, own_far, near, near_far, far, far_far,
        w_time, b_time.reshape(1, -1), w_up, b_up.reshape(1, -1),
    )


def solution(mesh):
    placed = (
        P(("videos", "tm"), None, "tile", None),
        P(("videos", "tm")),
        P("videos"),
        P(),
        P(),
        P(),
        P(),
    )
    return jax.shard_map(
        per_device,
        mesh=mesh,
        in_specs=placed,
        out_specs=P(("videos", "tm"), None, "tile"),
        check_vma=False,
    )
```

```python
import jax
import jax.numpy as jnp
from jax import lax
from jax.experimental import pallas as pl
from jax.experimental.pallas import tpu as pltpu
from jax.sharding import PartitionSpec as P

OV = 4
F32 = jnp.float32
BF16 = jnp.bfloat16
VMEM = pl.BlockSpec(memory_space=pltpu.VMEM)
SMEM = pl.BlockSpec(memory_space=pltpu.SMEM)
ANY = pl.BlockSpec(memory_space=pl.ANY)
PARAMS = pltpu.CompilerParams(vmem_limit_bytes=24 << 20)


def dot(a, b):
    return jnp.dot(a, b, preferred_element_type=F32)


def dot_t(a, b):
    return lax.dot_general(a, b, (((1,), (1,)), ((), ())), preferred_element_type=F32)


def cost(flops, moved):
    return pl.CostEstimate(flops=flops, bytes_accessed=moved, transcendentals=0)


def prepare_weights(w_up, wc, wl, wr):
    outc, chans = w_up.shape[2], w_up.shape[3]
    pad = wl.shape[1] - outc
    for pr, block, rows in ((0, 0, (0,)), (0, 1, (1, 2)), (1, 0, (0, 1)), (1, 1, (2,))):
        taps = []
        for col in range(3):
            tap = w_up[rows[0], col].astype(F32)
            for row in rows[1:]:
                tap = tap + w_up[row, col].astype(F32)
            taps.append(tap)
        span = pl.ds(block * chans, chans)
        wc[pr, pl.ds(0, outc), span] = (taps[1] + taps[2]).astype(BF16)
        wc[pr, pl.ds(outc, outc), span] = (taps[0] + taps[1]).astype(BF16)
        wl[pr, pl.ds(0, outc), span] = taps[0].astype(BF16)
        wl[pr, pl.ds(outc, pad), span] = jnp.zeros((pad, chans), BF16)
        wr[pr, pl.ds(0, pad), span] = jnp.zeros((pad, chans), BF16)
        wr[pr, pl.ds(pad, outc), span] = taps[2].astype(BF16)


def placement(rows, cols):
    height, depth = 3 * cols * 2 * rows, 2 * rows * cols
    i = lax.broadcasted_iota(jnp.int32, (height, depth), 0)
    k = lax.broadcasted_iota(jnp.int32, (height, depth), 1)
    group = cols * 2 * rows
    shift = i // group
    col = (i % group) // (2 * rows)
    half = (i % (2 * rows)) // rows
    row = i % rows + shift - 1
    hit = (k == half * rows * cols + row * cols + col) & (row >= 0) & (row < rows)
    return jnp.where(hit, 1.0, 0.0).astype(BF16)


def picker(rows, cols, col):
    i = lax.broadcasted_iota(jnp.int32, (2 * rows, rows * cols), 0)
    k = lax.broadcasted_iota(jnp.int32, (2 * rows, rows * cols), 1)
    return jnp.where((i < rows) & (k == i * cols + col), 1.0, 0.0).astype(BF16)


def row_shifts(t):
    row = lax.broadcasted_iota(jnp.int32, t.shape, 0)
    up = jnp.where(row == 0, 0.0, pltpu.roll(t, 1, 0))
    down = jnp.where(row == t.shape[0] - 1, 0.0, pltpu.roll(t, t.shape[0] - 1, 0))
    return up, t, down


def fill_x(t, mine, place, x, rows, cols):
    chans = t.shape[1] // 2
    pixels = rows * cols
    body = t[:pixels].astype(BF16)
    both = jnp.concatenate([body[:, :chans], body[:, chans:]], 0)
    height = 2 * pixels
    edge = t[pixels : pixels + rows].astype(BF16).astype(F32)
    for v, shifted in enumerate(row_shifts(edge)):
        lanes = pl.ds(v * chans, chans)
        x[pl.ds(2 * rows, height), lanes] = dot(place[pl.ds(v * height, height), :], both).astype(BF16)
        column = jnp.concatenate([shifted[:, :chans], shifted[:, chans:]], 0)
        x[pl.ds(0, 2 * rows), lanes] = jnp.where(mine == 1, column, 0.0).astype(BF16)
        x[pl.ds(2 * rows + height, 2 * rows), lanes] = jnp.where(mine == 0, column, 0.0).astype(BF16)


def convolve(x, wc, wl, wr, b_up, owners, mine, wide, out, rows, cols):
    chans2 = wc.shape[2]
    chans = chans2 // 2
    height = 2 * rows * cols
    lanes = wc.shape[1]
    part = wl.shape[1]
    col_of = lax.broadcasted_iota(jnp.int32, (height, 1), 0) // (2 * rows)
    strip_from = jnp.where(mine == 0, cols - OV, 0)
    soft = 1.0 - 0.5 / (2 * OV)
    scale_l = jnp.where(col_of == strip_from, soft, 1.0)
    scale_r = jnp.where(col_of == strip_from + OV - 1, soft, 1.0)
    bias = jnp.concatenate([b_up[...], b_up[...]], -1)
    for pr in range(2):
        span = pl.ds(pr * chans, chans2)
        mid = dot_t(x[pl.ds(2 * rows, height), span], wc[pr])
        left = dot_t(x[pl.ds(0, height), span], wl[pr]) * scale_l
        right = dot_t(x[pl.ds(4 * rows, height), span], wr[pr]) * scale_r
        low = mid[:, : lanes - part] + left[:, : lanes - part]
        centre = mid[:, lanes - part : part] + left[:, lanes - part :] + right[:, : 2 * part - lanes]
        high = mid[:, part:] + right[:, 2 * part - lanes :]
        y = jnp.concatenate([low, centre, high], -1) + bias
        for col in range(cols):
            for h in range(2):
                top = col * 2 * rows + h * rows
                for j in range(lanes // 128):
                    wide[h, col * lanes // 128 + j, pl.ds(pr, rows, stride=2), :] = y[
                        top : top + rows, j * 128 : (j + 1) * 128
                    ]
    out_row = lax.broadcasted_iota(jnp.int32, (2 * rows, 128), 0)
    keep = jnp.zeros((2 * rows, 128), jnp.int32)
    for r in range(2 * rows):
        keep = jnp.where(out_row == r, owners[r], keep)
    keep = keep == mine
    for col in range(cols):
        shared = col < OV or col >= cols - OV
        outside = (col < strip_from) | (col >= strip_from + OV)
        for h in range(2):
            for lane in range(col * lanes, (col + 1) * lanes, 128):
                block = wide[h, lane // 128]
                if shared:
                    block = jnp.where(keep | outside, block, 0.0)
                out[h, :, pl.ds(lane, 128)] = block.astype(BF16)


def pack_kernel(frame_counts, own, own_far, to_far, to_near):
    slots, rows, cols, chans = own.shape
    pixels = rows * cols
    mine = lax.axis_index("tile")
    two = frame_counts[0] >= 2
    latest = jnp.where(two, own[1].reshape(pixels, chans), own[0].reshape(pixels, chans))
    latest_far = jnp.where(two, own_far[1].reshape(pixels, chans), own_far[0].reshape(pixels, chans))
    theirs = picker(rows, cols, jnp.where(mine == 0, OV, cols - OV - 1))
    edge = picker(rows, cols, jnp.where(mine == 0, cols - OV - 1, OV))
    to_far[pl.ds(0, pixels), :] = latest
    to_far[pl.ds(pixels, 2 * rows), :] = dot(theirs, latest_far).astype(BF16)
    to_near[pl.ds(0, 2 * rows), :] = dot(edge, own[0].reshape(pixels, chans)).astype(BF16)
    to_near[pl.ds(2 * rows, 2 * rows), :] = dot(edge, own[1].reshape(pixels, chans)).astype(BF16)
    mark = jnp.where(two, 2.0, 1.0)
    to_near[pl.ds(4 * rows, 2 * rows), :] = jnp.full((2 * rows, chans), mark, F32).astype(BF16)


def local_kernel(own, own_far, w_time, b_time, w_up, t0, t1, place, wc, wl, wr, lhs):
    slots, rows, cols, chans = own.shape
    pixels = rows * cols
    mine = lax.axis_index("tile")
    pick = picker(rows, cols, jnp.where(mine == 0, OV, cols - OV - 1))
    for k in range(2):
        lhs[k, pl.ds(0, pixels), :] = own[k].reshape(pixels, chans)
        lhs[k, pl.ds(pixels, 2 * rows), :] = dot(pick, own_far[k].reshape(pixels, chans)).astype(BF16)
    t0[...] = b_time[...] + dot(lhs[0], w_time[2])
    t1[...] = b_time[...] + dot(lhs[1], w_time[2]) + dot(lhs[0], w_time[1])
    place[...] = placement(rows, cols)
    prepare_weights(w_up, wc, wl, wr)


def near_is_two(edges, rows):
    return jnp.max(edges[pl.ds(4 * rows, 2 * rows), :].astype(F32)) > 1.5


def near_kernel(
    frame_counts, owners, near, edges, w_time, b_up, t0, t1, place, wc, wl, wr, out, t0_new, lhs, x, wide
):
    slots, rows, cols, chans = near.shape
    pixels = rows * cols
    mine = lax.axis_index("tile")
    first = lax.axis_index("tm") == 0
    two = near_is_two(edges, rows)
    newer = jnp.where(two, near[1].reshape(pixels, chans), near[0].reshape(pixels, chans))
    newer_far = jnp.where(two, edges[pl.ds(2 * rows, 2 * rows), :], edges[pl.ds(0, 2 * rows), :])
    lhs[pl.ds(0, pixels), :] = jnp.where(first, jnp.zeros_like(newer), newer)
    lhs[pl.ds(pixels, 2 * rows), :] = jnp.where(first, jnp.zeros_like(newer_far), newer_far)

    @pl.when(frame_counts[0] >= 2)
    def _():
        t = t1[...] + dot(lhs[...], w_time[0])
        fill_x(t, mine, place, x, rows, cols)
        convolve(x, wc, wl, wr, b_up, owners, mine, wide, out, rows, cols)

    @pl.when(frame_counts[0] < 2)
    def _():
        out[...] = jnp.zeros_like(out)

    t0_new[...] = t0[...] + dot(lhs[...], w_time[1])


def far_kernel(
    owners, near, edges, far, w_time, b_up, t0, place, wc, wl, wr, done, out, lhs, x, wide
):
    slots, rows, cols, chans = near.shape
    pixels = rows * cols
    mine = lax.axis_index("tile")
    place_tm = lax.axis_index("tm")
    two = near_is_two(edges, rows)
    older = jnp.where(two, near[0].reshape(pixels, chans), far[pl.ds(0, pixels), :])
    older_far = jnp.where(two, edges[pl.ds(0, 2 * rows), :], far[pl.ds(pixels, 2 * rows), :])
    none = (place_tm == 0) | ((place_tm == 1) & jnp.logical_not(two))
    lhs[pl.ds(0, pixels), :] = jnp.where(none, jnp.zeros_like(older), older)
    lhs[pl.ds(pixels, 2 * rows), :] = jnp.where(none, jnp.zeros_like(older_far), older_far)
    t = t0[...] + dot(lhs[...], w_time[0])
    fill_x(t, mine, place, x, rows, cols)
    convolve(x, wc, wl, wr, b_up, owners, mine, wide, out, rows, cols)


def per_device(latents, frame_counts, owners, w_time, b_time, w_up, b_up):
    slots, rows, cols, chans = latents.shape
    outc = w_up.shape[3]
    ring = lax.axis_size("tm")
    other = [(0, 1), (1, 0)]
    pixels, extra = rows * cols, 2 * rows
    lanes = 2 * cols * outc
    shape = jax.ShapeDtypeStruct

    def step(k):
        return [(i, (i + k) % ring) for i in range(ring)]

    def step_flip(k):
        return [(2 * i + t, 2 * ((i + k) % ring) + 1 - t) for i in range(ring) for t in range(2)]

    w_up = w_up.transpose(0, 1, 3, 2)
    b_time = b_time.reshape(1, -1)
    b_up = b_up.reshape(1, -1)
    near = lax.ppermute(latents, "tm", step(1))
    own_far = lax.ppermute(latents, "tile", other)
    to_far, to_near = pl.pallas_call(
        pack_kernel,
        out_shape=(shape((pixels + extra, chans), BF16), shape((3 * extra, chans), BF16)),
        in_specs=[SMEM, VMEM, VMEM],
        out_specs=(VMEM, VMEM),
        compiler_params=PARAMS,
        cost_estimate=cost(10**7, 600_000),
        name="pack",
    )(frame_counts, latents, own_far)
    far = lax.ppermute(to_far, "tm", step(2))
    edges = lax.ppermute(to_near, ("tm", "tile"), step_flip(1))
    partial = shape((pixels + extra, 2 * chans), F32)
    x_shape = pltpu.VMEM(((cols + 2) * extra, 3 * chans), BF16)
    wide_shape = pltpu.VMEM((2, lanes // 128, extra, 128), F32)
    t0, t1, place, wc, wl, wr = pl.pallas_call(
        local_kernel,
        out_shape=(
            partial,
            partial,
            shape((6 * pixels, 2 * pixels), BF16),
            shape((2, 2 * outc, 2 * chans), BF16),
            shape((2, 256, 2 * chans), BF16),
            shape((2, 256, 2 * chans), BF16),
        ),
        in_specs=[VMEM] * 5,
        out_specs=(VMEM,) * 6,
        scratch_shapes=[pltpu.VMEM((2, pixels + extra, chans), BF16)],
        compiler_params=PARAMS,
        cost_estimate=cost(6 * 10**8, 6 << 20),
        name="local",
    )(latents, own_far, w_time, b_time, w_up)
    out, t0 = pl.pallas_call(
        near_kernel,
        grid=(1,),
        out_shape=(shape((2 * slots, 2 * rows, lanes), BF16), partial),
        in_specs=[SMEM, SMEM] + [VMEM] * 10,
        out_specs=(pl.BlockSpec((2, 2 * rows, lanes), lambda i: (1, 0, 0)), VMEM),
        scratch_shapes=[pltpu.VMEM((pixels + extra, chans), BF16), x_shape, wide_shape],
        compiler_params=PARAMS,
        cost_estimate=cost(10**9, 4 << 20),
        name="near",
    )(frame_counts, owners, near, edges, w_time, b_up, t0, t1, place, wc, wl, wr)
    return pl.pallas_call(
        far_kernel,
        grid=(1,),
        out_shape=shape((2 * slots, 2 * rows, lanes), BF16),
        in_specs=[SMEM] + [VMEM] * 10 + [ANY],
        out_specs=pl.BlockSpec((2, 2 * rows, lanes), lambda i: (0, 0, 0)),
        scratch_shapes=[pltpu.VMEM((pixels + extra, chans), BF16), x_shape, wide_shape],
        input_output_aliases={11: 0},
        compiler_params=PARAMS,
        cost_estimate=cost(10**9, 4 << 20),
        name="far",
    )(owners, near, edges, far, w_time, b_up, t0, place, wc, wl, wr, out)


def solution(mesh):
    placed = (
        P(("videos", "tm"), None, "tile", None),
        P(("videos", "tm")),
        P("videos"),
        P(),
        P(),
        P(),
        P(),
    )
    return jax.shard_map(
        per_device,
        mesh=mesh,
        in_specs=placed,
        out_specs=P(("videos", "tm"), None, "tile"),
        check_vma=False,
    )
```

```python
import jax
import jax.numpy as jnp
from jax import lax
from jax.experimental import pallas as pl
from jax.experimental.pallas import tpu as pltpu
from jax.sharding import PartitionSpec as P

OV = 4
F32 = jnp.float32
BF16 = jnp.bfloat16
VMEM = pl.BlockSpec(memory_space=pltpu.VMEM)
SMEM = pl.BlockSpec(memory_space=pltpu.SMEM)
HBM = pl.BlockSpec(memory_space=pltpu.HBM)
LEAVES = 4
PARAMS = pltpu.CompilerParams(vmem_limit_bytes=24 << 20)


def dot(a, b):
    return jnp.dot(a, b, preferred_element_type=F32)


def dot_t(a, b):
    return lax.dot_general(a, b, (((1,), (1,)), ((), ())), preferred_element_type=F32)


def cost(flops, moved):
    return pl.CostEstimate(flops=flops, bytes_accessed=moved, transcendentals=0)


def prepare_weights(w_up, wc, wl, wr):
    outc, chans = w_up.shape[2], w_up.shape[3]
    pad = wl.shape[1] - outc
    for pr, block, rows in ((0, 0, (0,)), (0, 1, (1, 2)), (1, 0, (0, 1)), (1, 1, (2,))):
        taps = []
        for col in range(3):
            tap = w_up[rows[0], col].astype(F32)
            for row in rows[1:]:
                tap = tap + w_up[row, col].astype(F32)
            taps.append(tap)
        span = pl.ds(block * chans, chans)
        wc[pr, pl.ds(0, outc), span] = (taps[1] + taps[2]).astype(BF16)
        wc[pr, pl.ds(outc, outc), span] = (taps[0] + taps[1]).astype(BF16)
        wl[pr, pl.ds(0, outc), span] = taps[0].astype(BF16)
        wl[pr, pl.ds(outc, pad), span] = jnp.zeros((pad, chans), BF16)
        wr[pr, pl.ds(0, pad), span] = jnp.zeros((pad, chans), BF16)
        wr[pr, pl.ds(pad, outc), span] = taps[2].astype(BF16)


def placement(rows, cols):
    height, depth = 3 * cols * 2 * rows, 2 * rows * cols
    i = lax.broadcasted_iota(jnp.int32, (height, depth), 0)
    k = lax.broadcasted_iota(jnp.int32, (height, depth), 1)
    group = cols * 2 * rows
    shift = i // group
    col = (i % group) // (2 * rows)
    half = (i % (2 * rows)) // rows
    row = i % rows + shift - 1
    hit = (k == half * rows * cols + row * cols + col) & (row >= 0) & (row < rows)
    return jnp.where(hit, 1.0, 0.0).astype(BF16)


def picker(rows, cols, col):
    i = lax.broadcasted_iota(jnp.int32, (2 * rows, rows * cols), 0)
    k = lax.broadcasted_iota(jnp.int32, (2 * rows, rows * cols), 1)
    return jnp.where((i < rows) & (k == i * cols + col), 1.0, 0.0).astype(BF16)


def row_shifts(t):
    row = lax.broadcasted_iota(jnp.int32, t.shape, 0)
    up = jnp.where(row == 0, 0.0, pltpu.roll(t, 1, 0))
    down = jnp.where(row == t.shape[0] - 1, 0.0, pltpu.roll(t, t.shape[0] - 1, 0))
    return up, t, down


def fill_x(t, mine, place, x, rows, cols):
    chans = t.shape[1] // 2
    pixels = rows * cols
    body = t[:pixels].astype(BF16)
    both = jnp.concatenate([body[:, :chans], body[:, chans:]], 0)
    height = 2 * pixels
    edge = t[pixels : pixels + rows].astype(BF16).astype(F32)
    for v, shifted in enumerate(row_shifts(edge)):
        lanes = pl.ds(v * chans, chans)
        x[pl.ds(2 * rows, height), lanes] = dot(place[pl.ds(v * height, height), :], both).astype(BF16)
        column = jnp.concatenate([shifted[:, :chans], shifted[:, chans:]], 0)
        x[pl.ds(0, 2 * rows), lanes] = jnp.where(mine == 1, column, 0.0).astype(BF16)
        x[pl.ds(2 * rows + height, 2 * rows), lanes] = jnp.where(mine == 0, column, 0.0).astype(BF16)


def convolve(x, wc, wl, wr, b_up, keep, mine, wide, done, out, sems, rows, cols):
    chans2 = wc.shape[2]
    chans = chans2 // 2
    height = 2 * rows * cols
    lanes = wc.shape[1]
    part = wl.shape[1]
    col_of = lax.broadcasted_iota(jnp.int32, (height, 1), 0) // (2 * rows)
    strip_from = jnp.where(mine == 0, cols - OV, 0)
    soft = 1.0 - 0.5 / (2 * OV)
    scale_l = jnp.where(col_of == strip_from, soft, 1.0)
    scale_r = jnp.where(col_of == strip_from + OV - 1, soft, 1.0)
    bias = b_up[...].reshape(1, -1)
    bias = jnp.concatenate([bias, bias], -1)
    for pr in range(2):
        span = pl.ds(pr * chans, chans2)
        mid = dot_t(x[pl.ds(2 * rows, height), span], wc[pr])
        left = dot_t(x[pl.ds(0, height), span], wl[pr]) * scale_l
        right = dot_t(x[pl.ds(4 * rows, height), span], wr[pr]) * scale_r
        low = mid[:, : lanes - part] + left[:, : lanes - part]
        centre = mid[:, lanes - part : part] + left[:, lanes - part :] + right[:, : 2 * part - lanes]
        high = mid[:, part:] + right[:, 2 * part - lanes :]
        y = jnp.concatenate([low, centre, high], -1) + bias
        for col in range(cols):
            for h in range(2):
                top = col * 2 * rows + h * rows
                for j in range(lanes // 128):
                    wide[h, col * lanes // 128 + j, pl.ds(pr, rows, stride=2), :] = y[
                        top : top + rows, j * 128 : (j + 1) * 128
                    ]
    keep = keep[...] > 0.5
    copies = leave(done, out, sems)
    for col in range(cols):
        shared = col < OV or col >= cols - OV
        outside = (col < strip_from) | (col >= strip_from + OV)
        for h in range(2):
            for lane in range(col * lanes, (col + 1) * lanes, 128):
                block = wide[h, lane // 128]
                if shared:
                    block = jnp.where(keep | outside, block, 0.0)
                done[h, :, pl.ds(lane, 128)] = block.astype(BF16)
        if (col + 1) % (cols // LEAVES) == 0:
            copies[col // (cols // LEAVES)].start()


def leave(done, out, sems):
    width = done.shape[2] // LEAVES
    spans = [pl.ds(k * width, width) for k in range(LEAVES)]
    return [
        pltpu.make_async_copy(done.at[:, :, span], out.at[:, :, span], sems.at[k])
        for k, span in enumerate(spans)
    ]


def pack_kernel(
    counts, owners_hbm, own_hbm, own_far, w_time_hbm, w_up_hbm,
    to_far, to_near, keep, own, w_time, w_up, owners, sems,
):
    loads = [
        pltpu.make_async_copy(source, target, sems.at[k])
        for k, (source, target) in enumerate(
            [(own_hbm, own), (owners_hbm, owners)]
            + [(w_time_hbm.at[2 - k], w_time.at[2 - k]) for k in range(3)]
            + [(w_up_hbm.at[k], w_up.at[k]) for k in range(3)]
        )
    ]
    for load in loads:
        load.start()
    slots, rows, cols, chans = own.shape
    pixels = rows * cols
    mine = lax.axis_index("tile")
    theirs = picker(rows, cols, jnp.where(mine == 0, OV, cols - OV - 1))
    edge = picker(rows, cols, jnp.where(mine == 0, cols - OV - 1, OV))
    for load in loads[:2]:
        load.wait()
    two = counts[0] >= 2
    latest = jnp.where(two, own[1].reshape(pixels, chans), own[0].reshape(pixels, chans))
    latest_far = jnp.where(two, own_far[1].reshape(pixels, chans), own_far[0].reshape(pixels, chans))
    to_far[pl.ds(0, pixels), :] = latest
    to_far[pl.ds(pixels, 2 * rows), :] = dot(theirs, latest_far).astype(BF16)
    to_near[pl.ds(0, 2 * rows), :] = dot(edge, own[0].reshape(pixels, chans)).astype(BF16)
    to_near[pl.ds(2 * rows, 2 * rows), :] = dot(edge, own[1].reshape(pixels, chans)).astype(BF16)
    mark = jnp.where(two, 2.0, 1.0)
    to_near[pl.ds(4 * rows, 2 * rows), :] = jnp.full((2 * rows, chans), mark, F32).astype(BF16)
    out_row = lax.broadcasted_iota(jnp.int32, keep.shape, 0)
    owner = jnp.zeros(keep.shape, jnp.int32)
    for r in range(2 * rows):
        owner = jnp.where(out_row == r, owners[r], owner)
    keep[...] = jnp.where(owner == mine, 1.0, 0.0)
    for load in loads[2:]:
        load.wait()


def local_kernel(own, own_far, w_time, b_time, w_up, t0, t1, place, wc, wl, wr, lhs):
    slots, rows, cols, chans = own.shape
    pixels = rows * cols
    mine = lax.axis_index("tile")
    pick = picker(rows, cols, jnp.where(mine == 0, OV, cols - OV - 1))
    for k in range(2):
        lhs[k, pl.ds(0, pixels), :] = own[k].reshape(pixels, chans)
        lhs[k, pl.ds(pixels, 2 * rows), :] = dot(pick, own_far[k].reshape(pixels, chans)).astype(BF16)
    bias = b_time[...].reshape(1, -1)
    t0[...] = bias + dot(lhs[0], w_time[2])
    t1[...] = bias + dot(lhs[1], w_time[2]) + dot(lhs[0], w_time[1])
    place[...] = placement(rows, cols)
    prepare_weights(w_up, wc, wl, wr)


def is_two(marks, rows):
    return jnp.max(marks[pl.ds(4 * rows, 2 * rows), :].astype(F32)) > 1.5


def near_kernel(
    marks, keep, near, edges, w_time, b_up, t0, t1, place, wc, wl, wr, out, t0_new, lhs, x, wide, done, sems
):
    slots, rows, cols, chans = near.shape
    pixels = rows * cols
    mine = lax.axis_index("tile")
    first = lax.axis_index("tm") == 0
    two = is_two(edges, rows)
    newer = jnp.where(two, near[1].reshape(pixels, chans), near[0].reshape(pixels, chans))
    newer_far = jnp.where(two, edges[pl.ds(2 * rows, 2 * rows), :], edges[pl.ds(0, 2 * rows), :])
    lhs[pl.ds(0, pixels), :] = jnp.where(first, jnp.zeros_like(newer), newer)
    lhs[pl.ds(pixels, 2 * rows), :] = jnp.where(first, jnp.zeros_like(newer_far), newer_far)
    valid = is_two(marks, rows)

    @pl.when(valid)
    def _():
        t = t1[...] + dot(lhs[...], w_time[0])
        fill_x(t, mine, place, x, rows, cols)
        convolve(x, wc, wl, wr, b_up, keep, mine, wide, done, out.at[pl.ds(2, 2)], sems, rows, cols)

    @pl.when(jnp.logical_not(valid))
    def _():
        done[...] = jnp.zeros_like(done)
        for copy in leave(done, out.at[pl.ds(2, 2)], sems):
            copy.start()

    t0_new[...] = t0[...] + dot(lhs[...], w_time[1])
    for copy in leave(done, out.at[pl.ds(2, 2)], sems):
        copy.wait()


def far_kernel(
    keep, near, edges, far, w_time, b_up, t0, place, wc, wl, wr, before, out, lhs, x, wide, done, sems
):
    slots, rows, cols, chans = near.shape
    pixels = rows * cols
    mine = lax.axis_index("tile")
    place_tm = lax.axis_index("tm")
    two = is_two(edges, rows)
    older = jnp.where(two, near[0].reshape(pixels, chans), far[pl.ds(0, pixels), :])
    older_far = jnp.where(two, edges[pl.ds(0, 2 * rows), :], far[pl.ds(pixels, 2 * rows), :])
    none = (place_tm == 0) | ((place_tm == 1) & jnp.logical_not(two))
    lhs[pl.ds(0, pixels), :] = jnp.where(none, jnp.zeros_like(older), older)
    lhs[pl.ds(pixels, 2 * rows), :] = jnp.where(none, jnp.zeros_like(older_far), older_far)
    t = t0[...] + dot(lhs[...], w_time[0])
    fill_x(t, mine, place, x, rows, cols)
    convolve(x, wc, wl, wr, b_up, keep, mine, wide, done, out.at[pl.ds(0, 2)], sems, rows, cols)
    for copy in leave(done, out.at[pl.ds(0, 2)], sems):
        copy.wait()


def per_device(latents, frame_counts, owners, w_time, b_time, w_up, b_up):
    slots, rows, cols, chans = latents.shape
    outc = w_up.shape[3]
    ring = lax.axis_size("tm")
    other = [(0, 1), (1, 0)]
    pixels, extra = rows * cols, 2 * rows
    lanes = 2 * cols * outc
    shape = jax.ShapeDtypeStruct

    def step(k):
        return [(i, (i + k) % ring) for i in range(ring)]

    def step_flip(k):
        return [(2 * i + t, 2 * ((i + k) % ring) + 1 - t) for i in range(ring) for t in range(2)]

    def stay(v):
        return pltpu.with_memory_space_constraint(v, pltpu.HBM)

    w_up = w_up.transpose(0, 1, 3, 2)
    near = lax.ppermute(latents, "tm", step(1))
    own_far = lax.ppermute(latents, "tile", other)
    to_far, to_near, keep, own, w_time, w_up = pl.pallas_call(
        pack_kernel,
        out_shape=(
            shape((pixels + extra, chans), BF16),
            shape((3 * extra, chans), BF16),
            shape((extra, 128), F32),
            shape(latents.shape, BF16),
            shape(w_time.shape, BF16),
            shape(w_up.shape, BF16),
        ),
        in_specs=[SMEM, HBM, HBM, VMEM, HBM, HBM],
        out_specs=(VMEM,) * 6,
        scratch_shapes=[
            pltpu.SMEM(owners.shape, jnp.int32),
            pltpu.SemaphoreType.DMA((8,)),
        ],
        compiler_params=PARAMS,
        cost_estimate=cost(10**7, 4 << 20),
        name="pack",
    )(frame_counts, stay(owners), stay(latents), own_far, stay(w_time), stay(w_up))
    far = lax.ppermute(to_far, "tm", step(2))
    edges = lax.ppermute(to_near, ("tm", "tile"), step_flip(1))
    partial = shape((pixels + extra, 2 * chans), F32)
    scratch = [
        pltpu.VMEM((pixels + extra, chans), BF16),
        pltpu.VMEM(((cols + 2) * extra, 3 * chans), BF16),
        pltpu.VMEM((2, lanes // 128, extra, 128), F32),
        pltpu.VMEM((2, extra, lanes), BF16),
        pltpu.SemaphoreType.DMA((LEAVES,)),
    ]
    t0, t1, place, wc, wl, wr = pl.pallas_call(
        local_kernel,
        out_shape=(
            partial,
            partial,
            shape((6 * pixels, 2 * pixels), BF16),
            shape((2, 2 * outc, 2 * chans), BF16),
            shape((2, 256, 2 * chans), BF16),
            shape((2, 256, 2 * chans), BF16),
        ),
        in_specs=[VMEM] * 5,
        out_specs=(VMEM,) * 6,
        scratch_shapes=[pltpu.VMEM((2, pixels + extra, chans), BF16)],
        compiler_params=PARAMS,
        cost_estimate=cost(6 * 10**8, 6 << 20),
        name="local",
    )(own, own_far, w_time, b_time, w_up)
    out, t0 = pl.pallas_call(
        near_kernel,
        out_shape=(shape((2 * slots, 2 * rows, lanes), BF16), partial),
        in_specs=[VMEM] * 12,
        out_specs=(HBM, VMEM),
        scratch_shapes=scratch,
        compiler_params=PARAMS,
        cost_estimate=cost(10**9, 4 << 20),
        name="near",
    )(to_near, keep, near, edges, w_time, b_up, t0, t1, place, wc, wl, wr)
    return pl.pallas_call(
        far_kernel,
        out_shape=shape((2 * slots, 2 * rows, lanes), BF16),
        in_specs=[VMEM] * 11 + [HBM],
        out_specs=HBM,
        scratch_shapes=scratch,
        input_output_aliases={11: 0},
        compiler_params=PARAMS,
        cost_estimate=cost(10**9, 4 << 20),
        name="far",
    )(keep, near, edges, far, w_time, b_up, t0, place, wc, wl, wr, out)


def solution(mesh):
    placed = (
        P(("videos", "tm"), None, "tile", None),
        P(("videos", "tm")),
        P("videos"),
        P(),
        P(),
        P(),
        P(),
    )
    return jax.shard_map(
        per_device,
        mesh=mesh,
        in_specs=placed,
        out_specs=P(("videos", "tm"), None, "tile"),
        check_vma=False,
    )
```

```python
import jax
import jax.numpy as jnp
from jax import lax
from jax.experimental import pallas as pl
from jax.experimental.pallas import tpu as pltpu
from jax.sharding import PartitionSpec as P

OV = 4
F32 = jnp.float32
BF16 = jnp.bfloat16
VMEM = pl.BlockSpec(memory_space=pltpu.VMEM)
SMEM = pl.BlockSpec(memory_space=pltpu.SMEM)
HBM = pl.BlockSpec(memory_space=pltpu.HBM)
LEAVES = 4
ABSENT = 16384.0
PARAMS = pltpu.CompilerParams(vmem_limit_bytes=24 << 20)


def dot(a, b):
    return jnp.dot(a, b, preferred_element_type=F32)


def dot_t(a, b):
    return lax.dot_general(a, b, (((1,), (1,)), ((), ())), preferred_element_type=F32)


def cost(flops, moved):
    return pl.CostEstimate(flops=flops, bytes_accessed=moved, transcendentals=0)


def prepare_weights(w_up, wc, wl, wr):
    outc, chans = w_up.shape[2], w_up.shape[3]
    pad = wl.shape[1] - outc
    for pr, block, rows in ((1, 1, (2,)), (0, 1, (1, 2)), (1, 0, (0, 1)), (0, 0, (0,))):
        taps = []
        for col in range(3):
            tap = w_up[rows[0], col].astype(F32)
            for row in rows[1:]:
                tap = tap + w_up[row, col].astype(F32)
            taps.append(tap)
        span = pl.ds(block * chans, chans)
        wc[pr, pl.ds(0, outc), span] = (taps[1] + taps[2]).astype(BF16)
        wc[pr, pl.ds(outc, outc), span] = (taps[0] + taps[1]).astype(BF16)
        wl[pr, pl.ds(0, outc), span] = taps[0].astype(BF16)
        wl[pr, pl.ds(outc, pad), span] = jnp.zeros((pad, chans), BF16)
        wr[pr, pl.ds(0, pad), span] = jnp.zeros((pad, chans), BF16)
        wr[pr, pl.ds(pad, outc), span] = taps[2].astype(BF16)


def turner(rows, cols):
    i = lax.broadcasted_iota(jnp.int32, (rows * cols, rows * cols), 0)
    k = lax.broadcasted_iota(jnp.int32, (rows * cols, rows * cols), 1)
    return jnp.where(k == (i % rows) * cols + i // rows, 1.0, 0.0).astype(BF16)


def picker(rows, cols, col):
    i = lax.broadcasted_iota(jnp.int32, (2 * rows, rows * cols), 0)
    k = lax.broadcasted_iota(jnp.int32, (2 * rows, rows * cols), 1)
    return jnp.where((i < rows) & (k == i * cols + col), 1.0, 0.0).astype(BF16)


def fill_x(t, mine, x, rows, cols):
    chans = t.shape[1] // 2
    t = t.astype(BF16).astype(F32)
    row = lax.broadcasted_iota(jnp.int32, (rows, 2 * chans), 0)
    for col in range(cols + 1):
        one = t[col * rows : (col + 1) * rows]
        up = jnp.where(row == 0, 0.0, pltpu.roll(one, 1, 0))
        down = jnp.where(row == rows - 1, 0.0, pltpu.roll(one, rows - 1, 0))
        for v, shifted in enumerate((up, one, down)):
            lanes = pl.ds(v * chans, chans)
            column = jnp.concatenate([shifted[:, :chans], shifted[:, chans:]], 0)
            if col < cols:
                x[pl.ds((col + 1) * 2 * rows, 2 * rows), lanes] = column.astype(BF16)
            else:
                x[pl.ds(0, 2 * rows), lanes] = jnp.where(mine == 1, column, 0.0).astype(BF16)
                x[pl.ds((cols + 1) * 2 * rows, 2 * rows), lanes] = jnp.where(mine == 0, column, 0.0).astype(BF16)


def convolve(x, wc, wl, wr, b_up, keep, mine, wide, done, rows, cols, copies):
    chans2 = wc.shape[2]
    chans = chans2 // 2
    height = 2 * rows * cols
    lanes = wc.shape[1]
    part = wl.shape[1]
    col_of = lax.broadcasted_iota(jnp.int32, (height, 1), 0) // (2 * rows)
    strip_from = jnp.where(mine == 0, cols - OV, 0)
    soft = 1.0 - 0.5 / (2 * OV)
    scale_l = jnp.where(col_of == strip_from, soft, 1.0)
    scale_r = jnp.where(col_of == strip_from + OV - 1, soft, 1.0)
    bias = b_up[...].reshape(1, -1)
    bias = jnp.concatenate([bias, bias], -1)
    for pr in range(2):
        span = pl.ds(pr * chans, chans2)
        mid = dot_t(x[pl.ds(2 * rows, height), span], wc[pr])
        left = dot_t(x[pl.ds(0, height), span], wl[pr]) * scale_l
        right = dot_t(x[pl.ds(4 * rows, height), span], wr[pr]) * scale_r
        low = mid[:, : lanes - part] + left[:, : lanes - part]
        centre = mid[:, lanes - part : part] + left[:, lanes - part :] + right[:, : 2 * part - lanes]
        high = mid[:, part:] + right[:, 2 * part - lanes :]
        y = jnp.concatenate([low, centre, high], -1) + bias
        for col in range(cols):
            for h in range(2):
                top = col * 2 * rows + h * rows
                for j in range(lanes // 128):
                    wide[h, col * lanes // 128 + j, pl.ds(pr, rows, stride=2), :] = y[
                        top : top + rows, j * 128 : (j + 1) * 128
                    ]
    keep = keep[...] > 0.5
    for col in range(cols):
        shared = col < OV or col >= cols - OV
        outside = (col < strip_from) | (col >= strip_from + OV)
        for h in range(2):
            for lane in range(col * lanes, (col + 1) * lanes, 128):
                block = wide[h, lane // 128]
                if shared:
                    block = jnp.where(keep | outside, block, 0.0)
                done[h, :, pl.ds(lane, 128)] = block.astype(BF16)
        if copies and (col + 1) % (cols // LEAVES) == 0:
            copies[col // (cols // LEAVES)].start()


def leave(done, out, sems):
    width = done.shape[2] // LEAVES
    spans = [pl.ds(k * width, width) for k in range(LEAVES)]
    return [
        pltpu.make_async_copy(done.at[:, :, span], out.at[:, :, span], sems.at[k])
        for k, span in enumerate(spans)
    ]


def load_kernel(owners_hbm, own_hbm, b_time_hbm, b_up_hbm, keep, own, b_time, b_up, owners, sems):
    pairs = [(own_hbm, own), (owners_hbm, owners), (b_time_hbm, b_time), (b_up_hbm, b_up)]
    loads = [pltpu.make_async_copy(source, target, sems.at[k]) for k, (source, target) in enumerate(pairs)]
    for load in loads:
        load.start()
    mine = lax.axis_index("tile")
    for load in loads:
        load.wait()
    out_row = lax.broadcasted_iota(jnp.int32, keep.shape, 0)
    owner = jnp.zeros(keep.shape, jnp.int32)
    for r in range(keep.shape[0]):
        owner = jnp.where(out_row == r, owners[r], owner)
    keep[...] = jnp.where(owner == mine, 1.0, 0.0)


def pack_kernel(counts, own, own_far, latest, before):
    slots, rows, cols, chans = own.shape
    pixels = rows * cols
    mine = lax.axis_index("tile")
    two = counts[0] >= 2
    turn = turner(rows, cols)
    pick = picker(rows, cols, jnp.where(mine == 0, OV, cols - OV - 1))
    first, second = own[0].reshape(pixels, chans), own[1].reshape(pixels, chans)
    first_far, second_far = own_far[0].reshape(pixels, chans), own_far[1].reshape(pixels, chans)
    latest[pl.ds(0, pixels), :] = dot(turn, jnp.where(two, second, first)).astype(BF16)
    latest[pl.ds(pixels, 2 * rows), :] = dot(pick, jnp.where(two, second_far, first_far)).astype(BF16)
    before[pl.ds(0, pixels), :] = jnp.where(two, dot(turn, first), ABSENT).astype(BF16)
    before[pl.ds(pixels, 2 * rows), :] = jnp.where(two, dot(pick, first_far), ABSENT).astype(BF16)


def local_kernel(latest, before, w_time, b_time, w_up, t0, t1, wc, wl, wr, lhs):
    two = is_there(before)
    lhs[...] = jnp.where(two, before[...], latest[...])
    prepare_weights(w_up, wc, wl, wr)
    bias = b_time[...].reshape(1, -1)
    t0[...] = bias + dot(lhs[...], w_time[2])

    @pl.when(two)
    def _():
        t1[...] = bias + dot(latest[...], w_time[2]) + dot(lhs[...], w_time[1])


def is_there(frame):
    return jnp.max(frame[pl.ds(0, 16), pl.ds(0, 128)].astype(F32)) < 0.5 * ABSENT


def near_kernel(before, keep, newer, w_time, b_up, t0, t1, wc, wl, wr, done, t0_new, lhs, x, wide):
    rows = keep.shape[0] // 2
    cols = (newer.shape[0] - 2 * rows) // rows
    mine = lax.axis_index("tile")
    lhs[...] = jnp.where(lax.axis_index("tm") == 0, jnp.zeros_like(newer), newer[...])
    valid = is_there(before)

    @pl.when(valid)
    def _():
        t = t1[...] + dot(lhs[...], w_time[0])
        fill_x(t, mine, x, rows, cols)
        convolve(x, wc, wl, wr, b_up, keep, mine, wide, done, rows, cols, [])

    @pl.when(jnp.logical_not(valid))
    def _():
        done[...] = jnp.zeros_like(done)

    t0_new[...] = t0[...] + dot(lhs[...], w_time[1])


def far_kernel(
    keep, near_before, far, w_time, b_up, t0, wc, wl, wr, second, out, lhs, x, wide, done, sems
):
    early = pltpu.make_async_copy(second, out.at[pl.ds(2, 2)], sems.at[LEAVES])
    early.start()
    rows = keep.shape[0] // 2
    cols = (far.shape[0] - 2 * rows) // rows
    mine = lax.axis_index("tile")
    place_tm = lax.axis_index("tm")
    two = is_there(near_before)
    older = jnp.where(two, near_before[...], far[...])
    none = (place_tm == 0) | ((place_tm == 1) & jnp.logical_not(two))
    lhs[...] = jnp.where(none, jnp.zeros_like(older), older)
    t = t0[...] + dot(lhs[...], w_time[0])
    fill_x(t, mine, x, rows, cols)
    copies = leave(done, out.at[pl.ds(0, 2)], sems)
    convolve(x, wc, wl, wr, b_up, keep, mine, wide, done, rows, cols, copies)
    for copy in copies + [early]:
        copy.wait()


def per_device(latents, frame_counts, owners, w_time, b_time, w_up, b_up):
    slots, rows, cols, chans = latents.shape
    outc = w_up.shape[3]
    ring = lax.axis_size("tm")
    pixels, extra = rows * cols, 2 * rows
    lanes = 2 * cols * outc
    shape = jax.ShapeDtypeStruct

    def step(k):
        return [(i, (i + k) % ring) for i in range(ring)]

    def stay(v):
        return pltpu.with_memory_space_constraint(v, pltpu.HBM)

    w_up = w_up.transpose(0, 1, 3, 2)
    own_far = lax.ppermute(latents, "tile", [(0, 1), (1, 0)])
    keep, own, b_time, b_up = pl.pallas_call(
        load_kernel,
        out_shape=(
            shape((extra, 128), F32),
            shape(latents.shape, BF16),
            shape(b_time.shape, F32),
            shape(b_up.shape, F32),
        ),
        in_specs=[HBM] * 4,
        out_specs=(VMEM,) * 4,
        scratch_shapes=[pltpu.SMEM(owners.shape, jnp.int32), pltpu.SemaphoreType.DMA((4,))],
        compiler_params=PARAMS,
        cost_estimate=cost(10**6, 1 << 10),
        name="load",
    )(stay(owners), stay(latents), stay(b_time), stay(b_up))
    frame = shape((pixels + extra, chans), BF16)
    latest, before = pl.pallas_call(
        pack_kernel,
        out_shape=(frame, frame),
        in_specs=[SMEM, VMEM, VMEM],
        out_specs=(VMEM,) * 2,
        compiler_params=PARAMS,
        cost_estimate=cost(3 * 10**9, 1 << 10),
        name="pack",
    )(frame_counts, own, own_far)
    newer = lax.ppermute(latest, "tm", step(1))
    far = lax.ppermute(latest, "tm", [(i, i + 2) for i in range(ring - 2)])
    near_before = lax.ppermute(before, "tm", step(1))
    partial = shape((pixels + extra, 2 * chans), F32)
    scratch = [
        pltpu.VMEM(frame.shape, BF16),
        pltpu.VMEM(((cols + 2) * extra, 3 * chans), BF16),
        pltpu.VMEM((2, lanes // 128, extra, 128), F32),
        pltpu.VMEM((2, extra, lanes), BF16),
        pltpu.SemaphoreType.DMA((LEAVES + 1,)),
    ]
    t0, t1, wc, wl, wr = pl.pallas_call(
        local_kernel,
        out_shape=(
            partial,
            partial,
            shape((2, 2 * outc, 2 * chans), BF16),
            shape((2, 256, 2 * chans), BF16),
            shape((2, 256, 2 * chans), BF16),
        ),
        in_specs=[VMEM] * 5,
        out_specs=(VMEM,) * 5,
        scratch_shapes=[pltpu.VMEM(frame.shape, BF16)],
        compiler_params=PARAMS,
        cost_estimate=cost(10**6, 1 << 10),
        name="local",
    )(latest, before, w_time, b_time, w_up)
    second, t0 = pl.pallas_call(
        near_kernel,
        out_shape=(shape((2, 2 * rows, lanes), BF16), partial),
        in_specs=[VMEM] * 10,
        out_specs=(VMEM, VMEM),
        scratch_shapes=scratch[:3],
        compiler_params=PARAMS,
        cost_estimate=cost(10**9, 4 << 20),
        name="near",
    )(before, keep, newer, w_time, b_up, t0, t1, wc, wl, wr)
    return pl.pallas_call(
        far_kernel,
        out_shape=shape((2 * slots, 2 * rows, lanes), BF16),
        in_specs=[VMEM] * 10,
        out_specs=HBM,
        scratch_shapes=scratch,
        compiler_params=PARAMS,
        cost_estimate=cost(10**9, 4 << 20),
        name="far",
    )(keep, near_before, far, w_time, b_up, t0, wc, wl, wr, second)


def solution(mesh):
    placed = (
        P(("videos", "tm"), None, "tile", None),
        P(("videos", "tm")),
        P("videos"),
        P(),
        P(),
        P(),
        P(),
    )
    return jax.shard_map(
        per_device,
        mesh=mesh,
        in_specs=placed,
        out_specs=P(("videos", "tm"), None, "tile"),
        check_vma=False,
    )
```

```python
import jax
import jax.numpy as jnp
from jax import lax
from jax.experimental import pallas as pl
from jax.experimental.pallas import tpu as pltpu
from jax.sharding import PartitionSpec as P

OV = 4
F32 = jnp.float32
BF16 = jnp.bfloat16
VMEM = pl.BlockSpec(memory_space=pltpu.VMEM)
SMEM = pl.BlockSpec(memory_space=pltpu.SMEM)
HBM = pl.BlockSpec(memory_space=pltpu.HBM)
LEAVES = 4
ABSENT = 16384.0
PARAMS = pltpu.CompilerParams(vmem_limit_bytes=24 << 20)


def dot(a, b):
    return jnp.dot(a, b, preferred_element_type=F32)


def dot_t(a, b):
    return lax.dot_general(a, b, (((1,), (1,)), ((), ())), preferred_element_type=F32)


def cost(flops, moved):
    return pl.CostEstimate(flops=flops, bytes_accessed=moved, transcendentals=0)


def prepare_weights(w_up, wp):
    outc, chans = w_up.shape[2], w_up.shape[3]
    for pr, block, rows in ((1, 1, (2,)), (0, 1, (1, 2)), (1, 0, (0, 1)), (0, 0, (0,))):
        taps = []
        for col in range(3):
            tap = w_up[rows[0], col].astype(F32)
            for row in rows[1:]:
                tap = tap + w_up[row, col].astype(F32)
            taps.append(tap)
        for k, tap in enumerate((taps[1] + taps[2], taps[0] + taps[1], taps[0], taps[2])):
            wp[pr, pl.ds(k * outc, outc), pl.ds(block * chans, chans)] = tap.astype(BF16)


def turner(rows, cols):
    i = lax.broadcasted_iota(jnp.int32, (rows * cols, rows * cols), 0)
    k = lax.broadcasted_iota(jnp.int32, (rows * cols, rows * cols), 1)
    return jnp.where(k == (i % rows) * cols + i // rows, 1.0, 0.0).astype(BF16)


def picker(rows, cols, col):
    i = lax.broadcasted_iota(jnp.int32, (2 * rows, rows * cols), 0)
    k = lax.broadcasted_iota(jnp.int32, (2 * rows, rows * cols), 1)
    return jnp.where((i < rows) & (k == i * cols + col), 1.0, 0.0).astype(BF16)


def fill_x(t, mine, x, rows, cols):
    chans = t.shape[1] // 2
    t = t.astype(BF16).astype(F32)
    row = lax.broadcasted_iota(jnp.int32, (rows, 2 * chans), 0)
    for col in range(cols + 1):
        one = t[col * rows : (col + 1) * rows]
        up = jnp.where(row == 0, 0.0, pltpu.roll(one, 1, 0))
        down = jnp.where(row == rows - 1, 0.0, pltpu.roll(one, rows - 1, 0))
        for v, shifted in enumerate((up, one, down)):
            lanes = pl.ds(v * chans, chans)
            column = jnp.concatenate([shifted[:, :chans], shifted[:, chans:]], 0)
            if col < cols:
                x[pl.ds((col + 1) * 2 * rows, 2 * rows), lanes] = column.astype(BF16)
            else:
                x[pl.ds(0, 2 * rows), lanes] = jnp.where(mine == 1, column, 0.0).astype(BF16)
                x[pl.ds((cols + 1) * 2 * rows, 2 * rows), lanes] = jnp.where(mine == 0, column, 0.0).astype(BF16)


def convolve(x, wp, b_up, keep, mine, wide, done, rows, cols, copies):
    chans2 = wp.shape[2]
    chans = chans2 // 2
    column = 2 * rows
    outc = wp.shape[1] // 4
    lanes = 2 * outc
    strip_from = jnp.where(mine == 0, cols - OV, 0)
    soft = 1.0 - 0.5 / (2 * OV)
    bias = b_up[...].reshape(1, -1)
    bias = jnp.concatenate([bias, bias], -1)
    before_half = lax.broadcasted_iota(jnp.int32, (column, 128), 1) < outc % 128
    for pr in range(2):
        z = dot_t(x[:, pl.ds(pr * chans, chans2)], wp[pr])
        for col in range(cols):
            scale_l = scale_r = 1.0
            if col in (0, cols - OV):
                scale_l = jnp.where(strip_from == col, soft, 1.0)
            if col in (OV - 1, cols - 1):
                scale_r = jnp.where(strip_from + OV - 1 == col, soft, 1.0)
            here = z[(col + 1) * column : (col + 2) * column, :lanes] + bias
            prev = z[col * column : (col + 1) * column, lanes:] * scale_l
            after = z[(col + 2) * column : (col + 3) * column, lanes:] * scale_r
            tiles = []
            for j in range(lanes // 128):
                span = slice(j * 128, (j + 1) * 128)
                if (j + 1) * 128 <= outc:
                    add = prev[:, span]
                elif j * 128 >= outc:
                    add = after[:, span]
                else:
                    add = jnp.where(before_half, prev[:, span], after[:, span])
                tiles.append(here[:, span] + add)
            for h in range(2):
                for j, tile in enumerate(tiles):
                    wide[h, col * lanes // 128 + j, pl.ds(pr, rows, stride=2), :] = tile[h * rows : (h + 1) * rows]
    keep = keep[...] > 0.5
    for col in range(cols):
        shared = col < OV or col >= cols - OV
        outside = (col < strip_from) | (col >= strip_from + OV)
        for h in range(2):
            for lane in range(col * lanes, (col + 1) * lanes, 128):
                block = wide[h, lane // 128]
                if shared:
                    block = jnp.where(keep | outside, block, 0.0)
                done[h, :, pl.ds(lane, 128)] = block.astype(BF16)
        if copies and (col + 1) % (cols // LEAVES) == 0:
            copies[col // (cols // LEAVES)].start()


def leave(done, out, sems):
    width = done.shape[2] // LEAVES
    spans = [pl.ds(k * width, width) for k in range(LEAVES)]
    return [
        pltpu.make_async_copy(done.at[:, :, span], out.at[:, :, span], sems.at[k])
        for k, span in enumerate(spans)
    ]


def load_kernel(owners_hbm, own_hbm, b_time_hbm, b_up_hbm, keep, own, b_time, b_up, owners, sems):
    pairs = [(own_hbm, own), (owners_hbm, owners), (b_time_hbm, b_time), (b_up_hbm, b_up)]
    loads = [pltpu.make_async_copy(source, target, sems.at[k]) for k, (source, target) in enumerate(pairs)]
    for load in loads:
        load.start()
    mine = lax.axis_index("tile")
    for load in loads:
        load.wait()
    out_row = lax.broadcasted_iota(jnp.int32, keep.shape, 0)
    owner = jnp.zeros(keep.shape, jnp.int32)
    for r in range(keep.shape[0]):
        owner = jnp.where(out_row == r, owners[r], owner)
    keep[...] = jnp.where(owner == mine, 1.0, 0.0)


def pack_kernel(counts, own, own_far, latest, before):
    slots, rows, cols, chans = own.shape
    pixels = rows * cols
    mine = lax.axis_index("tile")
    two = counts[0] >= 2
    turn = turner(rows, cols)
    pick = picker(rows, cols, jnp.where(mine == 0, OV, cols - OV - 1))
    first, second = own[0].reshape(pixels, chans), own[1].reshape(pixels, chans)
    first_far, second_far = own_far[0].reshape(pixels, chans), own_far[1].reshape(pixels, chans)
    latest[pl.ds(0, pixels), :] = dot(turn, jnp.where(two, second, first)).astype(BF16)
    latest[pl.ds(pixels, 2 * rows), :] = dot(pick, jnp.where(two, second_far, first_far)).astype(BF16)
    before[pl.ds(0, pixels), :] = jnp.where(two, dot(turn, first), ABSENT).astype(BF16)
    before[pl.ds(pixels, 2 * rows), :] = jnp.where(two, dot(pick, first_far), ABSENT).astype(BF16)


def local_kernel(latest, before, w_time, b_time, w_up, t0, t1, wp, lhs):
    two = is_there(before)
    lhs[...] = jnp.where(two, before[...], latest[...])
    prepare_weights(w_up, wp)
    bias = b_time[...].reshape(1, -1)
    t0[...] = bias + dot(lhs[...], w_time[2])

    @pl.when(two)
    def _():
        t1[...] = bias + dot(latest[...], w_time[2]) + dot(lhs[...], w_time[1])


def is_there(frame):
    return jnp.max(frame[pl.ds(0, 16), pl.ds(0, 128)].astype(F32)) < 0.5 * ABSENT


def near_kernel(before, keep, newer, w_time, b_up, t1, wp, done, lhs, x, wide):
    rows = keep.shape[0] // 2
    cols = (newer.shape[0] - 2 * rows) // rows
    mine = lax.axis_index("tile")
    lhs[...] = jnp.where(lax.axis_index("tm") == 0, jnp.zeros_like(newer), newer[...])
    valid = is_there(before)

    @pl.when(valid)
    def _():
        t = t1[...] + dot(lhs[...], w_time[0])
        fill_x(t, mine, x, rows, cols)
        convolve(x, wp, b_up, keep, mine, wide, done, rows, cols, [])

    @pl.when(jnp.logical_not(valid))
    def _():
        done[...] = jnp.zeros_like(done)


def far_kernel(
    keep, newer, near_before, far, w_time, b_up, t0, wp, second, out, lhs, x, wide, done, sems
):
    early = pltpu.make_async_copy(second, out.at[pl.ds(2, 2)], sems.at[LEAVES])
    early.start()
    rows = keep.shape[0] // 2
    cols = (far.shape[0] - 2 * rows) // rows
    mine = lax.axis_index("tile")
    place_tm = lax.axis_index("tm")
    two = is_there(near_before)
    older = jnp.where(two, near_before[...], far[...])
    none = (place_tm == 0) | ((place_tm == 1) & jnp.logical_not(two))
    chans = older.shape[1]
    lhs[:, pl.ds(0, chans)] = jnp.where(none, jnp.zeros_like(older), older)
    lhs[:, pl.ds(chans, chans)] = jnp.where(place_tm == 0, jnp.zeros_like(older), newer[...])
    t = t0[...] + dot(lhs[...], w_time[pl.ds(0, 2)].reshape(2 * chans, 2 * chans))
    fill_x(t, mine, x, rows, cols)
    copies = leave(done, out.at[pl.ds(0, 2)], sems)
    convolve(x, wp, b_up, keep, mine, wide, done, rows, cols, copies)
    for copy in copies + [early]:
        copy.wait()


def per_device(latents, frame_counts, owners, w_time, b_time, w_up, b_up):
    slots, rows, cols, chans = latents.shape
    outc = w_up.shape[3]
    ring = lax.axis_size("tm")
    pixels, extra = rows * cols, 2 * rows
    lanes = 2 * cols * outc
    shape = jax.ShapeDtypeStruct

    def step(k):
        return [(i, (i + k) % ring) for i in range(ring)]

    def stay(v):
        return pltpu.with_memory_space_constraint(v, pltpu.HBM)

    w_up = w_up.transpose(0, 1, 3, 2)
    own_far = lax.ppermute(latents, "tile", [(0, 1), (1, 0)])
    keep, own, b_time, b_up = pl.pallas_call(
        load_kernel,
        out_shape=(
            shape((extra, 128), F32),
            shape(latents.shape, BF16),
            shape(b_time.shape, F32),
            shape(b_up.shape, F32),
        ),
        in_specs=[HBM] * 4,
        out_specs=(VMEM,) * 4,
        scratch_shapes=[pltpu.SMEM(owners.shape, jnp.int32), pltpu.SemaphoreType.DMA((4,))],
        compiler_params=PARAMS,
        cost_estimate=cost(10**6, 1 << 10),
        name="load",
    )(stay(owners), stay(latents), stay(b_time), stay(b_up))
    frame = shape((pixels + extra, chans), BF16)
    latest, before = pl.pallas_call(
        pack_kernel,
        out_shape=(frame, frame),
        in_specs=[SMEM, VMEM, VMEM],
        out_specs=(VMEM,) * 2,
        compiler_params=PARAMS,
        cost_estimate=cost(3 * 10**9, 1 << 10),
        name="pack",
    )(frame_counts, own, own_far)
    newer = lax.ppermute(latest, "tm", step(1))
    far = lax.ppermute(latest, "tm", step(2))
    near_before = lax.ppermute(before, "tm", [(i, i + 1) for i in range(ring - 1)])
    partial = shape((pixels + extra, 2 * chans), F32)
    scratch = [
        pltpu.VMEM((pixels + extra, 2 * chans), BF16),
        pltpu.VMEM(((cols + 2) * extra, 3 * chans), BF16),
        pltpu.VMEM((2, lanes // 128, extra, 128), F32),
        pltpu.VMEM((2, extra, lanes), BF16),
        pltpu.SemaphoreType.DMA((LEAVES + 1,)),
    ]
    t0, t1, wp = pl.pallas_call(
        local_kernel,
        out_shape=(
            partial,
            partial,
            shape((2, 4 * outc, 2 * chans), BF16),
        ),
        in_specs=[VMEM] * 5,
        out_specs=(VMEM,) * 3,
        scratch_shapes=[pltpu.VMEM(frame.shape, BF16)],
        compiler_params=PARAMS,
        cost_estimate=cost(10**6, 1 << 10),
        name="local",
    )(latest, before, w_time, b_time, w_up)
    second = pl.pallas_call(
        near_kernel,
        out_shape=shape((2, 2 * rows, lanes), BF16),
        in_specs=[VMEM] * 7,
        out_specs=VMEM,
        scratch_shapes=[pltpu.VMEM(frame.shape, BF16)] + scratch[1:3],
        compiler_params=PARAMS,
        cost_estimate=cost(10**9, 4 << 20),
        name="near",
    )(before, keep, newer, w_time, b_up, t1, wp)
    return pl.pallas_call(
        far_kernel,
        out_shape=shape((2 * slots, 2 * rows, lanes), BF16),
        in_specs=[VMEM] * 9,
        out_specs=HBM,
        scratch_shapes=scratch,
        compiler_params=PARAMS,
        cost_estimate=cost(10**9, 4 << 20),
        name="far",
    )(keep, newer, near_before, far, w_time, b_up, t0, wp, second)


def solution(mesh):
    placed = (
        P(("videos", "tm"), None, "tile", None),
        P(("videos", "tm")),
        P("videos"),
        P(),
        P(),
        P(),
        P(),
    )
    return jax.shard_map(
        per_device,
        mesh=mesh,
        in_specs=placed,
        out_specs=P(("videos", "tm"), None, "tile"),
        check_vma=False,
    )
```

```python
import jax
import jax.numpy as jnp
from jax import lax
from jax.experimental import pallas as pl
from jax.experimental.pallas import tpu as pltpu
from jax.sharding import PartitionSpec as P

OV = 4
F32 = jnp.float32
BF16 = jnp.bfloat16
VMEM = pl.BlockSpec(memory_space=pltpu.VMEM)
SMEM = pl.BlockSpec(memory_space=pltpu.SMEM)
HBM = pl.BlockSpec(memory_space=pltpu.HBM)
LEAVES = 4
ABSENT = 16384.0
PARAMS = pltpu.CompilerParams(vmem_limit_bytes=24 << 20)


def dot(a, b):
    return jnp.dot(a, b, preferred_element_type=F32)


def dot_t(a, b):
    return lax.dot_general(a, b, (((1,), (1,)), ((), ())), preferred_element_type=F32)


def cost(flops, moved):
    return pl.CostEstimate(flops=flops, bytes_accessed=moved, transcendentals=0)


def prepare_weights(w_up, wp):
    outc, chans = w_up.shape[2], w_up.shape[3]
    for pr, block, rows in ((1, 1, (2,)), (0, 1, (1, 2)), (1, 0, (0, 1)), (0, 0, (0,))):
        taps = []
        for col in range(3):
            tap = w_up[rows[0], col].astype(F32)
            for row in rows[1:]:
                tap = tap + w_up[row, col].astype(F32)
            taps.append(tap)
        for k, tap in enumerate((taps[1] + taps[2], taps[0] + taps[1], taps[0], taps[2])):
            wp[pr, pl.ds(k * outc, outc), pl.ds(block * chans, chans)] = tap.astype(BF16)


def turner(rows, cols):
    i = lax.broadcasted_iota(jnp.int32, (rows * cols, rows * cols), 0)
    k = lax.broadcasted_iota(jnp.int32, (rows * cols, rows * cols), 1)
    return jnp.where(k == (i % rows) * cols + i // rows, 1.0, 0.0).astype(BF16)


def picker(rows, cols, col):
    i = lax.broadcasted_iota(jnp.int32, (rows, rows * cols), 0)
    k = lax.broadcasted_iota(jnp.int32, (rows, rows * cols), 1)
    return jnp.where(k == i * cols + col, 1.0, 0.0).astype(BF16)


def fill_x(t, mine, x, rows, cols):
    chans = t.shape[1] // 2
    t = t.astype(BF16).astype(F32)
    row = lax.broadcasted_iota(jnp.int32, (rows, 2 * chans), 0)
    for col in range(cols + 1):
        one = t[col * rows : (col + 1) * rows]
        up = jnp.where(row == 0, 0.0, pltpu.roll(one, 1, 0))
        down = jnp.where(row == rows - 1, 0.0, pltpu.roll(one, rows - 1, 0))
        for v, shifted in enumerate((up, one, down)):
            lanes = pl.ds(v * chans, chans)
            column = jnp.concatenate([shifted[:, :chans], shifted[:, chans:]], 0)
            if col < cols:
                x[pl.ds((col + 1) * 2 * rows, 2 * rows), lanes] = column.astype(BF16)
            else:
                x[pl.ds(0, 2 * rows), lanes] = jnp.where(mine == 1, column, 0.0).astype(BF16)
                x[pl.ds((cols + 1) * 2 * rows, 2 * rows), lanes] = jnp.where(mine == 0, column, 0.0).astype(BF16)


def convolve(x, wp, b_up, keep, mine, wide, done, rows, cols, copies):
    chans2 = wp.shape[2]
    chans = chans2 // 2
    column = 2 * rows
    outc = wp.shape[1] // 4
    lanes = 2 * outc
    strip_from = jnp.where(mine == 0, cols - OV, 0)
    soft = 1.0 - 0.5 / (2 * OV)
    bias = b_up[...].reshape(1, -1)
    bias = jnp.concatenate([bias, bias], -1)
    before_half = lax.broadcasted_iota(jnp.int32, (column, 128), 1) < outc % 128
    for pr in range(2):
        z = dot_t(x[:, pl.ds(pr * chans, chans2)], wp[pr])
        for col in range(cols):
            scale_l = scale_r = 1.0
            if col in (0, cols - OV):
                scale_l = jnp.where(strip_from == col, soft, 1.0)
            if col in (OV - 1, cols - 1):
                scale_r = jnp.where(strip_from + OV - 1 == col, soft, 1.0)
            here = z[(col + 1) * column : (col + 2) * column, :lanes] + bias
            prev = z[col * column : (col + 1) * column, lanes:] * scale_l
            after = z[(col + 2) * column : (col + 3) * column, lanes:] * scale_r
            tiles = []
            for j in range(lanes // 128):
                span = slice(j * 128, (j + 1) * 128)
                if (j + 1) * 128 <= outc:
                    add = prev[:, span]
                elif j * 128 >= outc:
                    add = after[:, span]
                else:
                    add = jnp.where(before_half, prev[:, span], after[:, span])
                tiles.append(here[:, span] + add)
            for h in range(2):
                for j, tile in enumerate(tiles):
                    wide[h, col * lanes // 128 + j, pl.ds(pr, rows, stride=2), :] = tile[h * rows : (h + 1) * rows]
    keep = keep[...] > 0.5
    for col in range(cols):
        shared = col < OV or col >= cols - OV
        outside = (col < strip_from) | (col >= strip_from + OV)
        for h in range(2):
            for lane in range(col * lanes, (col + 1) * lanes, 128):
                block = wide[h, lane // 128]
                if shared:
                    block = jnp.where(keep | outside, block, 0.0)
                done[h, :, pl.ds(lane, 128)] = block.astype(BF16)
        if copies and (col + 1) % (cols // LEAVES) == 0:
            copies[col // (cols // LEAVES)].start()


def leave(done, out, sems):
    width = done.shape[2] // LEAVES
    spans = [pl.ds(k * width, width) for k in range(LEAVES)]
    return [
        pltpu.make_async_copy(done.at[:, :, span], out.at[:, :, span], sems.at[k])
        for k, span in enumerate(spans)
    ]


def load_kernel(owners_hbm, own_hbm, b_time_hbm, b_up_hbm, keep, own, b_time, b_up, owners, sems):
    pairs = [(own_hbm, own), (owners_hbm, owners), (b_time_hbm, b_time), (b_up_hbm, b_up)]
    loads = [pltpu.make_async_copy(source, target, sems.at[k]) for k, (source, target) in enumerate(pairs)]
    for load in loads:
        load.start()
    mine = lax.axis_index("tile")
    for load in loads:
        load.wait()
    out_row = lax.broadcasted_iota(jnp.int32, keep.shape, 0)
    owner = jnp.zeros(keep.shape, jnp.int32)
    for r in range(keep.shape[0]):
        owner = jnp.where(out_row == r, owners[r], owner)
    keep[...] = jnp.where(owner == mine, 1.0, 0.0)


def pack_kernel(counts, own, own_far, latest, before):
    slots, rows, cols, chans = own.shape
    pixels = rows * cols
    mine = lax.axis_index("tile")
    two = counts[0] >= 2
    turn = turner(rows, cols)
    pick = picker(rows, cols, jnp.where(mine == 0, OV, cols - OV - 1))
    first, second = own[0].reshape(pixels, chans), own[1].reshape(pixels, chans)
    first_far, second_far = own_far[0].reshape(pixels, chans), own_far[1].reshape(pixels, chans)
    latest[pl.ds(0, pixels), :] = dot(turn, jnp.where(two, second, first)).astype(BF16)
    latest[pl.ds(pixels, rows), :] = dot(pick, jnp.where(two, second_far, first_far)).astype(BF16)
    before[pl.ds(0, pixels), :] = jnp.where(two, dot(turn, first), ABSENT).astype(BF16)
    before[pl.ds(pixels, rows), :] = jnp.where(two, dot(pick, first_far), ABSENT).astype(BF16)


def local_kernel(latest, before, w_time, b_time, w_up, t0, t1, wp, lhs):
    two = is_there(before)
    lhs[...] = jnp.where(two, before[...], latest[...])
    prepare_weights(w_up, wp)
    bias = b_time[...].reshape(1, -1)
    t0[...] = bias + dot(lhs[...], w_time[2])

    @pl.when(two)
    def _():
        t1[...] = bias + dot(latest[...], w_time[2]) + dot(lhs[...], w_time[1])


def is_there(frame):
    return jnp.max(frame[:16, :128].astype(F32)) < 0.5 * ABSENT


def near_kernel(before, keep, newer, w_time, b_up, t1, wp, done, lhs, x, wide):
    rows = keep.shape[0] // 2
    cols = newer.shape[0] // rows - 1
    mine = lax.axis_index("tile")
    lhs[...] = jnp.where(lax.axis_index("tm") == 0, jnp.zeros_like(newer), newer[...])
    valid = is_there(before)

    @pl.when(valid)
    def _():
        t = t1[...] + dot(lhs[...], w_time[0])
        fill_x(t, mine, x, rows, cols)
        convolve(x, wp, b_up, keep, mine, wide, done, rows, cols, [])

    @pl.when(jnp.logical_not(valid))
    def _():
        done[...] = jnp.zeros_like(done)


def far_kernel(
    keep, newer, near_before, far, w_time, b_up, t0, wp, second,
    out, lhs, x, wide, done, sems,
):
    early = pltpu.make_async_copy(second, out.at[pl.ds(2, 2)], sems.at[LEAVES])
    early.start()
    rows = keep.shape[0] // 2
    cols = far.shape[0] // rows - 1
    mine = lax.axis_index("tile")
    place_tm = lax.axis_index("tm")
    two = is_there(near_before)
    older = jnp.where(two, near_before[...], far[...])
    none = (place_tm == 0) | ((place_tm == 1) & jnp.logical_not(two))
    chans = older.shape[1]
    lhs[:, pl.ds(0, chans)] = jnp.where(none, jnp.zeros_like(older), older)
    lhs[:, pl.ds(chans, chans)] = jnp.where(place_tm == 0, jnp.zeros_like(older), newer[...])
    t = t0[...] + dot(lhs[...], w_time[pl.ds(0, 2)].reshape(2 * chans, 2 * chans))
    fill_x(t, mine, x, rows, cols)
    copies = leave(done, out.at[pl.ds(0, 2)], sems)
    convolve(x, wp, b_up, keep, mine, wide, done, rows, cols, copies)
    for copy in copies + [early]:
        copy.wait()


def per_device(latents, frame_counts, owners, w_time, b_time, w_up, b_up):
    slots, rows, cols, chans = latents.shape
    outc = w_up.shape[3]
    ring = lax.axis_size("tm")
    pixels, extra = rows * cols, 2 * rows
    lanes = 2 * cols * outc
    shape = jax.ShapeDtypeStruct

    def step(k):
        return [(i, (i + k) % ring) for i in range(ring)]

    def stay(v):
        return pltpu.with_memory_space_constraint(v, pltpu.HBM)

    w_up = w_up.transpose(0, 1, 3, 2)
    own_far = lax.ppermute(latents, "tile", [(0, 1), (1, 0)])
    keep, own, b_time, b_up = pl.pallas_call(
        load_kernel,
        out_shape=(
            shape((extra, 128), F32),
            shape(latents.shape, BF16),
            shape(b_time.shape, F32),
            shape(b_up.shape, F32),
        ),
        in_specs=[HBM] * 4,
        out_specs=(VMEM,) * 4,
        scratch_shapes=[pltpu.SMEM(owners.shape, jnp.int32), pltpu.SemaphoreType.DMA((4,))],
        compiler_params=PARAMS,
        cost_estimate=cost(10**6, 1 << 10),
        name="load",
    )(stay(owners), stay(latents), stay(b_time), stay(b_up))
    frame = shape((pixels + rows, chans), BF16)
    latest, before = pl.pallas_call(
        pack_kernel,
        out_shape=(frame, frame),
        in_specs=[SMEM, VMEM, VMEM],
        out_specs=(VMEM,) * 2,
        compiler_params=PARAMS,
        cost_estimate=cost(3 * 10**9, 1 << 10),
        name="pack",
    )(frame_counts, own, own_far)
    newer = lax.ppermute(latest, "tm", step(1))
    far = lax.ppermute(latest, "tm", step(2))
    near_before = lax.ppermute(before, "tm", [(i, i + 1) for i in range(ring - 1)])
    partial = shape((pixels + rows, 2 * chans), F32)
    scratch = [
        pltpu.VMEM((pixels + rows, 2 * chans), BF16),
        pltpu.VMEM(((cols + 2) * extra, 3 * chans), BF16),
        pltpu.VMEM((2, lanes // 128, extra, 128), F32),
        pltpu.VMEM((2, extra, lanes), BF16),
        pltpu.SemaphoreType.DMA((LEAVES + 1,)),
    ]
    t0, t1, wp = pl.pallas_call(
        local_kernel,
        out_shape=(
            partial,
            partial,
            shape((2, 4 * outc, 2 * chans), BF16),
        ),
        in_specs=[VMEM] * 5,
        out_specs=(VMEM,) * 3,
        scratch_shapes=[pltpu.VMEM(frame.shape, BF16)],
        compiler_params=PARAMS,
        cost_estimate=cost(10**6, 1 << 10),
        name="local",
    )(latest, before, w_time, b_time, w_up)
    second = pl.pallas_call(
        near_kernel,
        out_shape=shape((2, 2 * rows, lanes), BF16),
        in_specs=[VMEM] * 7,
        out_specs=VMEM,
        scratch_shapes=[pltpu.VMEM(frame.shape, BF16)] + scratch[1:3],
        compiler_params=PARAMS,
        cost_estimate=cost(10**9, 4 << 20),
        name="near",
    )(before, keep, newer, w_time, b_up, t1, wp)
    return pl.pallas_call(
        far_kernel,
        out_shape=shape((2 * slots, 2 * rows, lanes), BF16),
        in_specs=[VMEM] * 9,
        out_specs=HBM,
        scratch_shapes=scratch,
        compiler_params=PARAMS,
        cost_estimate=cost(10**9, 4 << 20),
        name="far",
    )(keep, newer, near_before, far, w_time, b_up, t0, wp, second)


def solution(mesh):
    placed = (
        P(("videos", "tm"), None, "tile", None),
        P(("videos", "tm")),
        P("videos"),
        P(),
        P(),
        P(),
        P(),
    )
    return jax.shard_map(
        per_device,
        mesh=mesh,
        in_specs=placed,
        out_specs=P(("videos", "tm"), None, "tile"),
        check_vma=False,
    )
```

```python
import jax
import jax.numpy as jnp
from jax import lax
from jax.experimental import pallas as pl
from jax.experimental.pallas import tpu as pltpu
from jax.sharding import PartitionSpec as P

OV = 4
F32 = jnp.float32
BF16 = jnp.bfloat16
VMEM = pl.BlockSpec(memory_space=pltpu.VMEM)
SMEM = pl.BlockSpec(memory_space=pltpu.SMEM)
HBM = pl.BlockSpec(memory_space=pltpu.HBM)
LEAVES = 4
ABSENT = 16384.0
PARAMS = pltpu.CompilerParams(vmem_limit_bytes=24 << 20)


def dot(a, b):
    return jnp.dot(a, b, preferred_element_type=F32)


def dot_t(a, b):
    return lax.dot_general(a, b, (((1,), (1,)), ((), ())), preferred_element_type=F32)


def cost(flops, moved):
    return pl.CostEstimate(flops=flops, bytes_accessed=moved, transcendentals=0)


def prepare_weights(w_up, wp):
    outc, chans = w_up.shape[2], w_up.shape[3]
    for pr, block, rows in ((1, 1, (2,)), (0, 1, (1, 2)), (1, 0, (0, 1)), (0, 0, (0,))):
        taps = []
        for col in range(3):
            tap = w_up[rows[0], col].astype(F32)
            for row in rows[1:]:
                tap = tap + w_up[row, col].astype(F32)
            taps.append(tap)
        for k, tap in enumerate((taps[1] + taps[2], taps[0] + taps[1], taps[0], taps[2])):
            wp[pr, pl.ds(k * outc, outc), pl.ds(block * chans, chans)] = tap.astype(BF16)


def turner(rows, cols):
    i = lax.broadcasted_iota(jnp.int32, (rows * cols, rows * cols), 0)
    k = lax.broadcasted_iota(jnp.int32, (rows * cols, rows * cols), 1)
    return jnp.where(k == (i % rows) * cols + i // rows, 1.0, 0.0).astype(BF16)


def picker(rows, cols, col):
    i = lax.broadcasted_iota(jnp.int32, (rows, rows * cols), 0)
    k = lax.broadcasted_iota(jnp.int32, (rows, rows * cols), 1)
    return jnp.where(k == i * cols + col, 1.0, 0.0).astype(BF16)


def fill_x(t, mine, x, rows, cols):
    chans = t.shape[1] // 2
    t = t.astype(BF16).astype(F32)
    row = lax.broadcasted_iota(jnp.int32, (rows, 2 * chans), 0)
    for col in range(cols + 1):
        one = t[col * rows : (col + 1) * rows]
        up = jnp.where(row == 0, 0.0, pltpu.roll(one, 1, 0))
        down = jnp.where(row == rows - 1, 0.0, pltpu.roll(one, rows - 1, 0))
        for v, shifted in enumerate((up, one, down)):
            lanes = pl.ds(v * chans, chans)
            column = jnp.concatenate([shifted[:, :chans], shifted[:, chans:]], 0)
            if col < cols:
                x[pl.ds((col + 1) * 2 * rows, 2 * rows), lanes] = column.astype(BF16)
            else:
                x[pl.ds(0, 2 * rows), lanes] = jnp.where(mine == 1, column, 0.0).astype(BF16)
                x[pl.ds((cols + 1) * 2 * rows, 2 * rows), lanes] = jnp.where(mine == 0, column, 0.0).astype(BF16)


def convolve(x, wp, b_up, keep, mine, wide, done, rows, cols, copies):
    chans2 = wp.shape[2]
    chans = chans2 // 2
    column = 2 * rows
    outc = wp.shape[1] // 4
    lanes = 2 * outc
    strip_from = jnp.where(mine == 0, cols - OV, 0)
    soft = 1.0 - 0.5 / (2 * OV)
    bias = b_up[...].reshape(1, -1)
    bias = jnp.concatenate([bias, bias], -1)
    before_half = lax.broadcasted_iota(jnp.int32, (column, 128), 1) < outc % 128
    for pr in range(2):
        z = dot_t(x[:, pl.ds(pr * chans, chans2)], wp[pr])
        for col in range(cols):
            scale_l = scale_r = 1.0
            if col in (0, cols - OV):
                scale_l = jnp.where(strip_from == col, soft, 1.0)
            if col in (OV - 1, cols - 1):
                scale_r = jnp.where(strip_from + OV - 1 == col, soft, 1.0)
            here = z[(col + 1) * column : (col + 2) * column, :lanes] + bias
            prev = z[col * column : (col + 1) * column, lanes:] * scale_l
            after = z[(col + 2) * column : (col + 3) * column, lanes:] * scale_r
            tiles = []
            for j in range(lanes // 128):
                span = slice(j * 128, (j + 1) * 128)
                if (j + 1) * 128 <= outc:
                    add = prev[:, span]
                elif j * 128 >= outc:
                    add = after[:, span]
                else:
                    add = jnp.where(before_half, prev[:, span], after[:, span])
                tiles.append(here[:, span] + add)
            for h in range(2):
                for j, tile in enumerate(tiles):
                    wide[h, col * lanes // 128 + j, pl.ds(pr, rows, stride=2), :] = tile[h * rows : (h + 1) * rows]
    keep = keep[...] > 0.5
    for col in range(cols):
        shared = col < OV or col >= cols - OV
        outside = (col < strip_from) | (col >= strip_from + OV)
        for h in range(2):
            for lane in range(col * lanes, (col + 1) * lanes, 128):
                block = wide[h, lane // 128]
                if shared:
                    block = jnp.where(keep | outside, block, 0.0)
                done[h, :, pl.ds(lane, 128)] = block.astype(BF16)
        if copies and (col + 1) % (cols // LEAVES) == 0:
            copies[col // (cols // LEAVES)].start()


def leave(done, out, sems):
    width = done.shape[2] // LEAVES
    spans = [pl.ds(k * width, width) for k in range(LEAVES)]
    return [
        pltpu.make_async_copy(done.at[:, :, span], out.at[:, :, span], sems.at[k])
        for k, span in enumerate(spans)
    ]


def load_kernel(owners_hbm, own_hbm, b_time_hbm, b_up_hbm, keep, own, b_time, b_up, owners, sems):
    pairs = [(owners_hbm, owners), (own_hbm, own), (b_time_hbm, b_time), (b_up_hbm, b_up)]
    loads = [pltpu.make_async_copy(source, target, sems.at[k]) for k, (source, target) in enumerate(pairs)]
    for load in loads:
        load.start()
    mine = lax.axis_index("tile")
    loads[0].wait()
    out_row = lax.broadcasted_iota(jnp.int32, keep.shape, 0)
    owner = jnp.zeros(keep.shape, jnp.int32)
    for r in range(keep.shape[0]):
        owner = jnp.where(out_row == r, owners[r], owner)
    keep[...] = jnp.where(owner == mine, 1.0, 0.0)
    for load in loads[1:]:
        load.wait()


def pack_kernel(counts, own, own_far, latest, before):
    slots, rows, cols, chans = own.shape
    pixels = rows * cols
    mine = lax.axis_index("tile")
    two = counts[0] >= 2
    turn = turner(rows, cols)
    pick = picker(rows, cols, jnp.where(mine == 0, OV, cols - OV - 1))
    first, second = own[0].reshape(pixels, chans), own[1].reshape(pixels, chans)
    first_far, second_far = own_far[0].reshape(pixels, chans), own_far[1].reshape(pixels, chans)
    latest[pl.ds(0, pixels), :] = dot(turn, jnp.where(two, second, first)).astype(BF16)
    latest[pl.ds(pixels, rows), :] = dot(pick, jnp.where(two, second_far, first_far)).astype(BF16)
    before[pl.ds(0, pixels), :] = jnp.where(two, dot(turn, first), ABSENT).astype(BF16)
    before[pl.ds(pixels, rows), :] = jnp.where(two, dot(pick, first_far), ABSENT).astype(BF16)


def local_kernel(counts, latest, before, w_time, b_time, w_up, t0, t1, wp, lhs):
    two = counts[0] >= 2
    lhs[...] = jnp.where(two, before[...], latest[...])
    prepare_weights(w_up, wp)
    bias = b_time[...].reshape(1, -1)
    t0[...] = bias + dot(lhs[...], w_time[2])

    @pl.when(two)
    def _():
        t1[...] = bias + dot(latest[...], w_time[2]) + dot(lhs[...], w_time[1])


def near_kernel(counts, before, keep, newer, w_time, b_up, t1, wp, done, lhs, x, wide):
    rows = keep.shape[0] // 2
    cols = newer.shape[0] // rows - 1
    mine = lax.axis_index("tile")
    lhs[...] = jnp.where(lax.axis_index("tm") == 0, jnp.zeros_like(newer), newer[...])
    valid = counts[0] >= 2

    @pl.when(valid)
    def _():
        t = t1[...] + dot(lhs[...], w_time[0])
        fill_x(t, mine, x, rows, cols)
        convolve(x, wp, b_up, keep, mine, wide, done, rows, cols, [])

    @pl.when(jnp.logical_not(valid))
    def _():
        done[...] = jnp.zeros_like(done)


def far_kernel(
    keep, newer, near_before, far, w_time, b_up, t0, wp, second,
    out, lhs, x, wide, done, sems,
):
    early = pltpu.make_async_copy(second, out.at[pl.ds(2, 2)], sems.at[LEAVES])
    early.start()
    rows = keep.shape[0] // 2
    cols = far.shape[0] // rows - 1
    mine = lax.axis_index("tile")
    place_tm = lax.axis_index("tm")
    chans = far.shape[1]
    nearer = near_before[...].astype(F32)
    further = jnp.where(place_tm >= 2, far[...].astype(F32), 0.0)
    older = jnp.where(nearer < 0.5 * ABSENT, nearer, further)
    lhs[:, pl.ds(0, chans)] = jnp.where(place_tm == 0, 0.0, older).astype(BF16)
    lhs[:, pl.ds(chans, chans)] = jnp.where(place_tm == 0, jnp.zeros_like(newer), newer[...])
    t = t0[...] + dot(lhs[...], w_time[pl.ds(0, 2)].reshape(2 * chans, 2 * chans))
    fill_x(t, mine, x, rows, cols)
    copies = leave(done, out.at[pl.ds(0, 2)], sems)
    convolve(x, wp, b_up, keep, mine, wide, done, rows, cols, copies)
    for copy in copies + [early]:
        copy.wait()


def per_device(latents, frame_counts, owners, w_time, b_time, w_up, b_up):
    slots, rows, cols, chans = latents.shape
    outc = w_up.shape[3]
    ring = lax.axis_size("tm")
    pixels, extra = rows * cols, 2 * rows
    lanes = 2 * cols * outc
    shape = jax.ShapeDtypeStruct

    def step(k):
        return [(i, (i + k) % ring) for i in range(ring)]

    def stay(v):
        return pltpu.with_memory_space_constraint(v, pltpu.HBM)

    w_up = w_up.transpose(0, 1, 3, 2)
    own_far = lax.ppermute(latents, "tile", [(0, 1), (1, 0)])
    keep, own, b_time, b_up = pl.pallas_call(
        load_kernel,
        out_shape=(
            shape((extra, 128), F32),
            shape(latents.shape, BF16),
            shape(b_time.shape, F32),
            shape(b_up.shape, F32),
        ),
        in_specs=[HBM] * 4,
        out_specs=(VMEM,) * 4,
        scratch_shapes=[pltpu.SMEM(owners.shape, jnp.int32), pltpu.SemaphoreType.DMA((4,))],
        compiler_params=PARAMS,
        cost_estimate=cost(10**6, 1 << 10),
        name="load",
    )(stay(owners), stay(latents), stay(b_time), stay(b_up))
    frame = shape((pixels + rows, chans), BF16)
    latest, before = pl.pallas_call(
        pack_kernel,
        out_shape=(frame, frame),
        in_specs=[SMEM, VMEM, VMEM],
        out_specs=(VMEM,) * 2,
        compiler_params=PARAMS,
        cost_estimate=cost(3 * 10**9, 1 << 10),
        name="pack",
    )(frame_counts, own, own_far)
    newer = lax.ppermute(latest, "tm", step(1))
    far = lax.ppermute(latest, "tm", step(2))
    near_before = lax.ppermute(before, "tm", [(i, i + 1) for i in range(ring - 1)])
    partial = shape((pixels + rows, 2 * chans), F32)
    scratch = [
        pltpu.VMEM((pixels + rows, 2 * chans), BF16),
        pltpu.VMEM(((cols + 2) * extra, 3 * chans), BF16),
        pltpu.VMEM((2, lanes // 128, extra, 128), F32),
        pltpu.VMEM((2, extra, lanes), BF16),
        pltpu.SemaphoreType.DMA((LEAVES + 1,)),
    ]
    t0, t1, wp = pl.pallas_call(
        local_kernel,
        out_shape=(
            partial,
            partial,
            shape((2, 4 * outc, 2 * chans), BF16),
        ),
        in_specs=[SMEM] + [VMEM] * 5,
        out_specs=(VMEM,) * 3,
        scratch_shapes=[pltpu.VMEM(frame.shape, BF16)],
        compiler_params=PARAMS,
        cost_estimate=cost(10**6, 1 << 10),
        name="local",
    )(frame_counts, latest, before, w_time, b_time, w_up)
    second = pl.pallas_call(
        near_kernel,
        out_shape=shape((2, 2 * rows, lanes), BF16),
        in_specs=[SMEM] + [VMEM] * 7,
        out_specs=VMEM,
        scratch_shapes=[pltpu.VMEM(frame.shape, BF16)] + scratch[1:3],
        compiler_params=PARAMS,
        cost_estimate=cost(10**9, 4 << 20),
        name="near",
    )(frame_counts, before, keep, newer, w_time, b_up, t1, wp)
    return pl.pallas_call(
        far_kernel,
        out_shape=shape((2 * slots, 2 * rows, lanes), BF16),
        in_specs=[VMEM] * 9,
        out_specs=HBM,
        scratch_shapes=scratch,
        compiler_params=PARAMS,
        cost_estimate=cost(10**9, 4 << 20),
        name="far",
    )(keep, newer, near_before, far, w_time, b_up, t0, wp, second)


def solution(mesh):
    placed = (
        P(("videos", "tm"), None, "tile", None),
        P(("videos", "tm")),
        P("videos"),
        P(),
        P(),
        P(),
        P(),
    )
    return jax.shard_map(
        per_device,
        mesh=mesh,
        in_specs=placed,
        out_specs=P(("videos", "tm"), None, "tile"),
        check_vma=False,
    )
```

```python
import jax
import jax.numpy as jnp
from jax import lax
from jax.experimental import pallas as pl
from jax.experimental.pallas import tpu as pltpu
from jax.sharding import PartitionSpec as P

OV = 4
F32 = jnp.float32
BF16 = jnp.bfloat16
VMEM = pl.BlockSpec(memory_space=pltpu.VMEM)
SMEM = pl.BlockSpec(memory_space=pltpu.SMEM)
HBM = pl.BlockSpec(memory_space=pltpu.HBM)
LEAVES = 4
ABSENT = 16384.0
PARAMS = pltpu.CompilerParams(vmem_limit_bytes=24 << 20)


def dot(a, b):
    return jnp.dot(a, b, preferred_element_type=F32)


def dot_t(a, b):
    return lax.dot_general(a, b, (((1,), (1,)), ((), ())), preferred_element_type=F32)


def cost(flops, moved):
    return pl.CostEstimate(flops=flops, bytes_accessed=moved, transcendentals=0)


def prepare_weights(w_up, wp):
    outc, chans = w_up.shape[2], w_up.shape[3]
    for pr, block, rows in ((1, 1, (2,)), (0, 1, (1, 2)), (1, 0, (0, 1)), (0, 0, (0,))):
        taps = []
        for col in range(3):
            tap = w_up[rows[0], col].astype(F32)
            for row in rows[1:]:
                tap = tap + w_up[row, col].astype(F32)
            taps.append(tap)
        for k, tap in enumerate((taps[1] + taps[2], taps[0] + taps[1], taps[0], taps[2])):
            wp[pr, pl.ds(k * outc, outc), pl.ds(block * chans, chans)] = tap.astype(BF16)


def turner(rows, cols):
    i = lax.broadcasted_iota(jnp.int32, (rows * cols, rows * cols), 0)
    k = lax.broadcasted_iota(jnp.int32, (rows * cols, rows * cols), 1)
    return jnp.where(k == (i % rows) * cols + i // rows, 1.0, 0.0).astype(BF16)


def picker(rows, cols, col):
    i = lax.broadcasted_iota(jnp.int32, (rows, rows * cols), 0)
    k = lax.broadcasted_iota(jnp.int32, (rows, rows * cols), 1)
    return jnp.where(k == i * cols + col, 1.0, 0.0).astype(BF16)


def fill_x(t, mine, x, rows, cols):
    chans = t.shape[1] // 2
    t = t.astype(BF16).astype(F32)
    row = lax.broadcasted_iota(jnp.int32, (rows, 2 * chans), 0)
    for col in range(cols + 1):
        one = t[col * rows : (col + 1) * rows]
        up = jnp.where(row == 0, 0.0, pltpu.roll(one, 1, 0))
        down = jnp.where(row == rows - 1, 0.0, pltpu.roll(one, rows - 1, 0))
        for v, shifted in enumerate((up, one, down)):
            lanes = pl.ds(v * chans, chans)
            column = jnp.concatenate([shifted[:, :chans], shifted[:, chans:]], 0)
            if col < cols:
                x[pl.ds((col + 1) * 2 * rows, 2 * rows), lanes] = column.astype(BF16)
            else:
                x[pl.ds(0, 2 * rows), lanes] = jnp.where(mine == 1, column, 0.0).astype(BF16)
                x[pl.ds((cols + 1) * 2 * rows, 2 * rows), lanes] = jnp.where(mine == 0, column, 0.0).astype(BF16)


def convolve(x, wp, b_up, keep, mine, wide, done, rows, cols, copies):
    chans2 = wp.shape[2]
    chans = chans2 // 2
    column = 2 * rows
    outc = wp.shape[1] // 4
    lanes = 2 * outc
    strip_from = jnp.where(mine == 0, cols - OV, 0)
    soft = 1.0 - 0.5 / (2 * OV)
    bias = b_up[...].reshape(1, -1)
    bias = jnp.concatenate([bias, bias], -1)
    before_half = lax.broadcasted_iota(jnp.int32, (column, 128), 1) < outc % 128
    for pr in range(2):
        z = dot_t(x[:, pl.ds(pr * chans, chans2)], wp[pr])
        for col in range(cols):
            scale_l = scale_r = 1.0
            if col in (0, cols - OV):
                scale_l = jnp.where(strip_from == col, soft, 1.0)
            if col in (OV - 1, cols - 1):
                scale_r = jnp.where(strip_from + OV - 1 == col, soft, 1.0)
            here = z[(col + 1) * column : (col + 2) * column, :lanes] + bias
            prev = z[col * column : (col + 1) * column, lanes:] * scale_l
            after = z[(col + 2) * column : (col + 3) * column, lanes:] * scale_r
            tiles = []
            for j in range(lanes // 128):
                span = slice(j * 128, (j + 1) * 128)
                if (j + 1) * 128 <= outc:
                    add = prev[:, span]
                elif j * 128 >= outc:
                    add = after[:, span]
                else:
                    add = jnp.where(before_half, prev[:, span], after[:, span])
                tiles.append(here[:, span] + add)
            for h in range(2):
                for j, tile in enumerate(tiles):
                    wide[h, col * lanes // 128 + j, pl.ds(pr, rows, stride=2), :] = tile[h * rows : (h + 1) * rows]
    keep = keep[...] > 0.5
    for col in range(cols):
        shared = col < OV or col >= cols - OV
        outside = (col < strip_from) | (col >= strip_from + OV)
        for h in range(2):
            for lane in range(col * lanes, (col + 1) * lanes, 128):
                block = wide[h, lane // 128]
                if shared:
                    block = jnp.where(keep | outside, block, 0.0)
                done[h, :, pl.ds(lane, 128)] = block.astype(BF16)
        if copies and (col + 1) % (cols // LEAVES) == 0:
            copies[col // (cols // LEAVES)].start()


def leave(done, out, sems):
    width = done.shape[2] // LEAVES
    spans = [pl.ds(k * width, width) for k in range(LEAVES)]
    return [
        pltpu.make_async_copy(done.at[:, :, span], out.at[:, :, span], sems.at[k])
        for k, span in enumerate(spans)
    ]


def load_kernel(owners_hbm, own_hbm, b_time_hbm, b_up_hbm, keep, own, b_time, b_up, owners, sems):
    pairs = [(owners_hbm, owners), (own_hbm, own), (b_time_hbm, b_time), (b_up_hbm, b_up)]
    loads = [pltpu.make_async_copy(source, target, sems.at[k]) for k, (source, target) in enumerate(pairs)]
    for load in loads:
        load.start()
    mine = lax.axis_index("tile")
    loads[0].wait()
    out_row = lax.broadcasted_iota(jnp.int32, keep.shape, 0)
    owner = jnp.zeros(keep.shape, jnp.int32)
    for r in range(keep.shape[0]):
        owner = jnp.where(out_row == r, owners[r], owner)
    keep[...] = jnp.where(owner == mine, 1.0, 0.0)
    for load in loads[1:]:
        load.wait()


def pack_kernel(counts, own, own_far, latest, before):
    slots, rows, cols, chans = own.shape
    pixels = rows * cols
    mine = lax.axis_index("tile")
    two = counts[0] >= 2
    turn = turner(rows, cols)
    pick = picker(rows, cols, jnp.where(mine == 0, OV, cols - OV - 1))
    first, second = own[0].reshape(pixels, chans), own[1].reshape(pixels, chans)
    first_far, second_far = own_far[0].reshape(pixels, chans), own_far[1].reshape(pixels, chans)
    latest[pl.ds(0, pixels), :] = dot(turn, jnp.where(two, second, first)).astype(BF16)
    latest[pl.ds(pixels, rows), :] = dot(pick, jnp.where(two, second_far, first_far)).astype(BF16)
    before[pl.ds(0, pixels), :] = jnp.where(two, dot(turn, first), ABSENT).astype(BF16)
    before[pl.ds(pixels, rows), :] = jnp.where(two, dot(pick, first_far), ABSENT).astype(BF16)


def local_kernel(counts, latest, before, w_time, b_time, w_up, t0, t1, wp, lhs):
    two = counts[0] >= 2
    lhs[...] = jnp.where(two, before[...], latest[...])
    prepare_weights(w_up, wp)
    bias = b_time[...].reshape(1, -1)
    t0[...] = bias + dot(lhs[...], w_time[2])

    @pl.when(two)
    def _():
        t1[...] = bias + dot(latest[...], w_time[2]) + dot(lhs[...], w_time[1])


def add_halo(later, t, frame, weight, total):
    @pl.when(later)
    def _():
        total[...] = t[...] + dot(frame[...], weight)

    @pl.when(jnp.logical_not(later))
    def _():
        total[...] = t[...]


def near_kernel(counts, before, keep, newer, w_time, b_up, t0, t1, wp, done, t0_new, total, x, wide):
    rows = keep.shape[0] // 2
    cols = newer.shape[0] // rows - 1
    mine = lax.axis_index("tile")
    later = lax.axis_index("tm") > 0
    valid = counts[0] >= 2

    @pl.when(valid)
    def _():
        add_halo(later, t1, newer, w_time[0], total)
        fill_x(total[...], mine, x, rows, cols)
        convolve(x, wp, b_up, keep, mine, wide, done, rows, cols, [])

    @pl.when(jnp.logical_not(valid))
    def _():
        done[...] = jnp.zeros_like(done)

    add_halo(later, t0, newer, w_time[1], t0_new)


def far_kernel(
    keep, far, near_before, w_time, b_up, t0, wp, second,
    out, lhs, total, x, wide, done, sems,
):
    early = pltpu.make_async_copy(second, out.at[pl.ds(2, 2)], sems.at[LEAVES])
    early.start()
    rows = keep.shape[0] // 2
    cols = far.shape[0] // rows - 1
    mine = lax.axis_index("tile")
    place_tm = lax.axis_index("tm")
    nearer = near_before[...].astype(F32)
    further = jnp.where(place_tm >= 2, far[...].astype(F32), 0.0)
    older = jnp.where(nearer < 0.5 * ABSENT, nearer, further)
    lhs[...] = older.astype(BF16)
    add_halo(place_tm > 0, t0, lhs, w_time[0], total)
    fill_x(total[...], mine, x, rows, cols)
    copies = leave(done, out.at[pl.ds(0, 2)], sems)
    convolve(x, wp, b_up, keep, mine, wide, done, rows, cols, copies)
    for copy in copies + [early]:
        copy.wait()


def per_device(latents, frame_counts, owners, w_time, b_time, w_up, b_up):
    slots, rows, cols, chans = latents.shape
    outc = w_up.shape[3]
    ring = lax.axis_size("tm")
    pixels, extra = rows * cols, 2 * rows
    lanes = 2 * cols * outc
    shape = jax.ShapeDtypeStruct

    def step(k):
        return [(i, (i + k) % ring) for i in range(ring)]

    def stay(v):
        return pltpu.with_memory_space_constraint(v, pltpu.HBM)

    w_up = w_up.transpose(0, 1, 3, 2)
    own_far = lax.ppermute(latents, "tile", [(0, 1), (1, 0)])
    keep, own, b_time, b_up = pl.pallas_call(
        load_kernel,
        out_shape=(
            shape((extra, 128), F32),
            shape(latents.shape, BF16),
            shape(b_time.shape, F32),
            shape(b_up.shape, F32),
        ),
        in_specs=[HBM] * 4,
        out_specs=(VMEM,) * 4,
        scratch_shapes=[pltpu.SMEM(owners.shape, jnp.int32), pltpu.SemaphoreType.DMA((4,))],
        compiler_params=PARAMS,
        cost_estimate=cost(10**6, 1 << 10),
        name="load",
    )(stay(owners), stay(latents), stay(b_time), stay(b_up))
    frame = shape((pixels + rows, chans), BF16)
    latest, before = pl.pallas_call(
        pack_kernel,
        out_shape=(frame, frame),
        in_specs=[SMEM, VMEM, VMEM],
        out_specs=(VMEM,) * 2,
        compiler_params=PARAMS,
        cost_estimate=cost(3 * 10**9, 1 << 10),
        name="pack",
    )(frame_counts, own, own_far)
    newer = lax.ppermute(latest, "tm", step(1))
    far = lax.ppermute(latest, "tm", step(2))
    near_before = lax.ppermute(before, "tm", [(i, i + 1) for i in range(ring - 1)])
    partial = shape((pixels + rows, 2 * chans), F32)
    scratch = [
        pltpu.VMEM(frame.shape, BF16),
        pltpu.VMEM(partial.shape, F32),
        pltpu.VMEM(((cols + 2) * extra, 3 * chans), BF16),
        pltpu.VMEM((2, lanes // 128, extra, 128), F32),
        pltpu.VMEM((2, extra, lanes), BF16),
        pltpu.SemaphoreType.DMA((LEAVES + 1,)),
    ]
    t0, t1, wp = pl.pallas_call(
        local_kernel,
        out_shape=(
            partial,
            partial,
            shape((2, 4 * outc, 2 * chans), BF16),
        ),
        in_specs=[SMEM] + [VMEM] * 5,
        out_specs=(VMEM,) * 3,
        scratch_shapes=[pltpu.VMEM(frame.shape, BF16)],
        compiler_params=PARAMS,
        cost_estimate=cost(10**6, 1 << 10),
        name="local",
    )(frame_counts, latest, before, w_time, b_time, w_up)
    second, t0 = pl.pallas_call(
        near_kernel,
        out_shape=(shape((2, 2 * rows, lanes), BF16), partial),
        in_specs=[SMEM] + [VMEM] * 8,
        out_specs=(VMEM, VMEM),
        scratch_shapes=[pltpu.VMEM(partial.shape, F32)] + scratch[2:4],
        compiler_params=PARAMS,
        cost_estimate=cost(10**9, 4 << 20),
        name="near",
    )(frame_counts, before, keep, newer, w_time, b_up, t0, t1, wp)
    return pl.pallas_call(
        far_kernel,
        out_shape=shape((2 * slots, 2 * rows, lanes), BF16),
        in_specs=[VMEM] * 8,
        out_specs=HBM,
        scratch_shapes=scratch,
        compiler_params=PARAMS,
        cost_estimate=cost(10**9, 4 << 20),
        name="far",
    )(keep, far, near_before, w_time, b_up, t0, wp, second)


def solution(mesh):
    placed = (
        P(("videos", "tm"), None, "tile", None),
        P(("videos", "tm")),
        P("videos"),
        P(),
        P(),
        P(),
        P(),
    )
    return jax.shard_map(
        per_device,
        mesh=mesh,
        in_specs=placed,
        out_specs=P(("videos", "tm"), None, "tile"),
        check_vma=False,
    )
```

```python
import jax
import jax.numpy as jnp
from jax import lax
from jax.experimental import pallas as pl
from jax.experimental.pallas import tpu as pltpu
from jax.sharding import PartitionSpec as P

OV = 4
F32 = jnp.float32
BF16 = jnp.bfloat16
VMEM = pl.BlockSpec(memory_space=pltpu.VMEM)
SMEM = pl.BlockSpec(memory_space=pltpu.SMEM)
HBM = pl.BlockSpec(memory_space=pltpu.HBM)
LEAVES = 4
ABSENT = 16384.0
PARAMS = pltpu.CompilerParams(vmem_limit_bytes=24 << 20)


def dot(a, b):
    return jnp.dot(a, b, preferred_element_type=F32)


def dot_t(a, b):
    return lax.dot_general(a, b, (((1,), (1,)), ((), ())), preferred_element_type=F32)


def cost(flops, moved):
    return pl.CostEstimate(flops=flops, bytes_accessed=moved, transcendentals=0)


def prepare_weights(w_up, wp):
    outc, chans = w_up.shape[2], w_up.shape[3]
    for pr, block, rows in ((1, 1, (2,)), (0, 1, (1, 2)), (1, 0, (0, 1)), (0, 0, (0,))):
        taps = []
        for col in range(3):
            tap = w_up[rows[0], col].astype(F32)
            for row in rows[1:]:
                tap = tap + w_up[row, col].astype(F32)
            taps.append(tap)
        for k, tap in enumerate((taps[1] + taps[2], taps[0] + taps[1], taps[0], taps[2])):
            start = k % 2 * outc
            for row in range(0, outc, 64):
                tile, inside = divmod(start + row, 128)
                target = tile * 256 + k // 2 * 128 + inside
                piece = tap[row : row + 64].astype(BF16)
                wp[pr, pl.ds(target, 64), pl.ds(block * chans, chans)] = piece


def turner(rows, cols):
    i = lax.broadcasted_iota(jnp.int32, (rows * cols, rows * cols), 0)
    k = lax.broadcasted_iota(jnp.int32, (rows * cols, rows * cols), 1)
    return jnp.where(k == (i % rows) * cols + i // rows, 1.0, 0.0).astype(BF16)


def picker(rows, cols, col):
    i = lax.broadcasted_iota(jnp.int32, (rows, rows * cols), 0)
    k = lax.broadcasted_iota(jnp.int32, (rows, rows * cols), 1)
    return jnp.where(k == i * cols + col, 1.0, 0.0).astype(BF16)


def fill_x(t, mine, x, rows, cols):
    chans = t.shape[1] // 2
    t = t.astype(BF16).astype(F32)
    row = lax.broadcasted_iota(jnp.int32, (rows, 2 * chans), 0)
    for col in range(cols + 1):
        one = t[col * rows : (col + 1) * rows]
        up = jnp.where(row == 0, 0.0, pltpu.roll(one, 1, 0))
        down = jnp.where(row == rows - 1, 0.0, pltpu.roll(one, rows - 1, 0))
        for v, shifted in enumerate((up, one, down)):
            lanes = pl.ds(v * chans, chans)
            column = jnp.concatenate([shifted[:, :chans], shifted[:, chans:]], 0)
            if col < cols:
                x[pl.ds((col + 1) * 2 * rows, 2 * rows), lanes] = column.astype(BF16)
            else:
                x[pl.ds(0, 2 * rows), lanes] = jnp.where(mine == 1, column, 0.0).astype(BF16)
                x[pl.ds((cols + 1) * 2 * rows, 2 * rows), lanes] = jnp.where(mine == 0, column, 0.0).astype(BF16)


def convolve(x, wp, b_up, keep, mine, wide, done, rows, cols, copies):
    chans2 = wp.shape[2]
    chans = chans2 // 2
    column = 2 * rows
    outc = wp.shape[1] // 4
    lanes = 2 * outc
    strip_from = jnp.where(mine == 0, cols - OV, 0)
    soft = 1.0 - 0.5 / (2 * OV)
    bias = b_up[...].reshape(1, -1)
    bias = jnp.concatenate([bias, bias], -1)
    before_half = lax.broadcasted_iota(jnp.int32, (column, 128), 1) < outc % 128
    for j in range(lanes // 128):
        for pr in range(2):
            z = dot_t(x[:, pl.ds(pr * chans, chans2)], wp[pr, pl.ds(j * 256, 256), :])
            for col in range(cols):
                scale_l = scale_r = 1.0
                if col in (0, cols - OV):
                    scale_l = jnp.where(strip_from == col, soft, 1.0)
                if col in (OV - 1, cols - 1):
                    scale_r = jnp.where(strip_from + OV - 1 == col, soft, 1.0)
                here = z[(col + 1) * column : (col + 2) * column, :128] + bias[:, j * 128 : (j + 1) * 128]
                prev = z[col * column : (col + 1) * column, 128:] * scale_l
                after = z[(col + 2) * column : (col + 3) * column, 128:] * scale_r
                if (j + 1) * 128 <= outc:
                    add = prev
                elif j * 128 >= outc:
                    add = after
                else:
                    add = jnp.where(before_half, prev, after)
                tile = here + add
                for h in range(2):
                    wide[h, col * lanes // 128 + j, pl.ds(pr, rows, stride=2), :] = tile[h * rows : (h + 1) * rows]
    keep = keep[...] > 0.5
    for col in range(cols):
        shared = col < OV or col >= cols - OV
        outside = (col < strip_from) | (col >= strip_from + OV)
        for h in range(2):
            for lane in range(col * lanes, (col + 1) * lanes, 128):
                block = wide[h, lane // 128]
                if shared:
                    block = jnp.where(keep | outside, block, 0.0)
                done[h, :, pl.ds(lane, 128)] = block.astype(BF16)
        if copies and (col + 1) % (cols // LEAVES) == 0:
            copies[col // (cols // LEAVES)].start()


def leave(done, out, sems):
    width = done.shape[2] // LEAVES
    spans = [pl.ds(k * width, width) for k in range(LEAVES)]
    return [
        pltpu.make_async_copy(done.at[:, :, span], out.at[:, :, span], sems.at[k])
        for k, span in enumerate(spans)
    ]


def load_kernel(owners_hbm, own_hbm, b_time_hbm, b_up_hbm, keep, own, b_time, b_up, owners, sems):
    pairs = [(owners_hbm, owners), (own_hbm, own), (b_time_hbm, b_time), (b_up_hbm, b_up)]
    loads = [pltpu.make_async_copy(source, target, sems.at[k]) for k, (source, target) in enumerate(pairs)]
    for load in loads:
        load.start()
    mine = lax.axis_index("tile")
    loads[0].wait()
    out_row = lax.broadcasted_iota(jnp.int32, keep.shape, 0)
    owner = jnp.zeros(keep.shape, jnp.int32)
    for r in range(keep.shape[0]):
        owner = jnp.where(out_row == r, owners[r], owner)
    keep[...] = jnp.where(owner == mine, 1.0, 0.0)
    for load in loads[1:]:
        load.wait()


def pack_kernel(counts, own, own_far, latest, before):
    slots, rows, cols, chans = own.shape
    pixels = rows * cols
    mine = lax.axis_index("tile")
    two = counts[0] >= 2
    turn = turner(rows, cols)
    pick = picker(rows, cols, jnp.where(mine == 0, OV, cols - OV - 1))
    first, second = own[0].reshape(pixels, chans), own[1].reshape(pixels, chans)
    first_far, second_far = own_far[0].reshape(pixels, chans), own_far[1].reshape(pixels, chans)
    latest[pl.ds(0, pixels), :] = dot(turn, jnp.where(two, second, first)).astype(BF16)
    latest[pl.ds(pixels, rows), :] = dot(pick, jnp.where(two, second_far, first_far)).astype(BF16)
    before[pl.ds(0, pixels), :] = jnp.where(two, dot(turn, first), ABSENT).astype(BF16)
    before[pl.ds(pixels, rows), :] = jnp.where(two, dot(pick, first_far), ABSENT).astype(BF16)


def local_kernel(counts, latest, before, w_time, b_time, w_up, t0, t1, wp, lhs):
    two = counts[0] >= 2
    lhs[...] = jnp.where(two, before[...], latest[...])
    prepare_weights(w_up, wp)
    bias = b_time[...].reshape(1, -1)
    t0[...] = bias + dot(lhs[...], w_time[2])

    @pl.when(two)
    def _():
        t1[...] = bias + dot(latest[...], w_time[2]) + dot(lhs[...], w_time[1])


def add_halo(later, t, frame, weight, total):
    @pl.when(later)
    def _():
        total[...] = t[...] + dot(frame[...], weight)

    @pl.when(jnp.logical_not(later))
    def _():
        total[...] = t[...]


def near_kernel(counts, before, keep, newer, w_time, b_up, t0, t1, wp, done, t0_new, total, x, wide):
    rows = keep.shape[0] // 2
    cols = newer.shape[0] // rows - 1
    mine = lax.axis_index("tile")
    later = lax.axis_index("tm") > 0
    valid = counts[0] >= 2

    @pl.when(valid)
    def _():
        add_halo(later, t1, newer, w_time[0], total)
        fill_x(total[...], mine, x, rows, cols)
        convolve(x, wp, b_up, keep, mine, wide, done, rows, cols, [])

    @pl.when(jnp.logical_not(valid))
    def _():
        done[...] = jnp.zeros_like(done)

    add_halo(later, t0, newer, w_time[1], t0_new)


def far_kernel(
    keep, far, near_before, w_time, b_up, t0, wp, second,
    out, lhs, total, x, wide, done, sems,
):
    early = pltpu.make_async_copy(second, out.at[pl.ds(2, 2)], sems.at[LEAVES])
    early.start()
    rows = keep.shape[0] // 2
    cols = far.shape[0] // rows - 1
    mine = lax.axis_index("tile")
    place_tm = lax.axis_index("tm")
    nearer = near_before[...].astype(F32)
    further = jnp.where(place_tm >= 2, far[...].astype(F32), 0.0)
    older = jnp.where(nearer < 0.5 * ABSENT, nearer, further)
    lhs[...] = older.astype(BF16)
    add_halo(place_tm > 0, t0, lhs, w_time[0], total)
    fill_x(total[...], mine, x, rows, cols)
    copies = leave(done, out.at[pl.ds(0, 2)], sems)
    convolve(x, wp, b_up, keep, mine, wide, done, rows, cols, copies)
    for copy in copies + [early]:
        copy.wait()


def per_device(latents, frame_counts, owners, w_time, b_time, w_up, b_up):
    slots, rows, cols, chans = latents.shape
    outc = w_up.shape[3]
    ring = lax.axis_size("tm")
    pixels, extra = rows * cols, 2 * rows
    lanes = 2 * cols * outc
    shape = jax.ShapeDtypeStruct

    def step(k):
        return [(i, (i + k) % ring) for i in range(ring)]

    def stay(v):
        return pltpu.with_memory_space_constraint(v, pltpu.HBM)

    w_up = w_up.transpose(0, 1, 3, 2)
    own_far = lax.ppermute(latents, "tile", [(0, 1), (1, 0)])
    keep, own, b_time, b_up = pl.pallas_call(
        load_kernel,
        out_shape=(
            shape((extra, 128), F32),
            shape(latents.shape, BF16),
            shape(b_time.shape, F32),
            shape(b_up.shape, F32),
        ),
        in_specs=[HBM] * 4,
        out_specs=(VMEM,) * 4,
        scratch_shapes=[pltpu.SMEM(owners.shape, jnp.int32), pltpu.SemaphoreType.DMA((4,))],
        compiler_params=PARAMS,
        cost_estimate=cost(10**6, 1 << 10),
        name="load",
    )(stay(owners), stay(latents), stay(b_time), stay(b_up))
    frame = shape((pixels + rows, chans), BF16)
    latest, before = pl.pallas_call(
        pack_kernel,
        out_shape=(frame, frame),
        in_specs=[SMEM, VMEM, VMEM],
        out_specs=(VMEM,) * 2,
        compiler_params=PARAMS,
        cost_estimate=cost(3 * 10**9, 1 << 10),
        name="pack",
    )(frame_counts, own, own_far)
    newer = lax.ppermute(latest, "tm", step(1))
    far = lax.ppermute(latest, "tm", step(2))
    near_before = lax.ppermute(before, "tm", [(i, i + 1) for i in range(ring - 1)])
    partial = shape((pixels + rows, 2 * chans), F32)
    scratch = [
        pltpu.VMEM(frame.shape, BF16),
        pltpu.VMEM(partial.shape, F32),
        pltpu.VMEM(((cols + 2) * extra, 3 * chans), BF16),
        pltpu.VMEM((2, lanes // 128, extra, 128), F32),
        pltpu.VMEM((2, extra, lanes), BF16),
        pltpu.SemaphoreType.DMA((LEAVES + 1,)),
    ]
    t0, t1, wp = pl.pallas_call(
        local_kernel,
        out_shape=(
            partial,
            partial,
            shape((2, 4 * outc, 2 * chans), BF16),
        ),
        in_specs=[SMEM] + [VMEM] * 5,
        out_specs=(VMEM,) * 3,
        scratch_shapes=[pltpu.VMEM(frame.shape, BF16)],
        compiler_params=PARAMS,
        cost_estimate=cost(10**6, 1 << 10),
        name="local",
    )(frame_counts, latest, before, w_time, b_time, w_up)
    second, t0 = pl.pallas_call(
        near_kernel,
        out_shape=(shape((2, 2 * rows, lanes), BF16), partial),
        in_specs=[SMEM] + [VMEM] * 8,
        out_specs=(VMEM, VMEM),
        scratch_shapes=[pltpu.VMEM(partial.shape, F32)] + scratch[2:4],
        compiler_params=PARAMS,
        cost_estimate=cost(10**9, 4 << 20),
        name="near",
    )(frame_counts, before, keep, newer, w_time, b_up, t0, t1, wp)
    return pl.pallas_call(
        far_kernel,
        out_shape=shape((2 * slots, 2 * rows, lanes), BF16),
        in_specs=[VMEM] * 8,
        out_specs=HBM,
        scratch_shapes=scratch,
        compiler_params=PARAMS,
        cost_estimate=cost(10**9, 4 << 20),
        name="far",
    )(keep, far, near_before, w_time, b_up, t0, wp, second)


def solution(mesh):
    placed = (
        P(("videos", "tm"), None, "tile", None),
        P(("videos", "tm")),
        P("videos"),
        P(),
        P(),
        P(),
        P(),
    )
    return jax.shard_map(
        per_device,
        mesh=mesh,
        in_specs=placed,
        out_specs=P(("videos", "tm"), None, "tile"),
        check_vma=False,
    )
```

```python
import jax
import jax.numpy as jnp
from jax import lax
from jax.experimental import pallas as pl
from jax.experimental.pallas import tpu as pltpu
from jax.sharding import PartitionSpec as P

OV = 4
F32 = jnp.float32
BF16 = jnp.bfloat16
VMEM = pl.BlockSpec(memory_space=pltpu.VMEM)
SMEM = pl.BlockSpec(memory_space=pltpu.SMEM)
HBM = pl.BlockSpec(memory_space=pltpu.HBM)
LEAVES = 4
ABSENT = 16384.0
PARAMS = pltpu.CompilerParams(vmem_limit_bytes=24 << 20)


def dot(a, b):
    return jnp.dot(a, b, preferred_element_type=F32)


def dot_t(a, b):
    return lax.dot_general(a, b, (((1,), (1,)), ((), ())), preferred_element_type=F32)


def cost(flops, moved):
    return pl.CostEstimate(flops=flops, bytes_accessed=moved, transcendentals=0)


def prepare_weights(w_up, wp):
    outc, chans = w_up.shape[2], w_up.shape[3]
    for pr, block, rows in ((1, 1, (2,)), (0, 1, (1, 2)), (1, 0, (0, 1)), (0, 0, (0,))):
        taps = []
        for col in range(3):
            tap = w_up[rows[0], col].astype(F32)
            for row in rows[1:]:
                tap = tap + w_up[row, col].astype(F32)
            taps.append(tap)
        for k, tap in enumerate((taps[1] + taps[2], taps[0] + taps[1], taps[0], taps[2])):
            start = k % 2 * outc
            for row in range(0, outc, 64):
                tile, inside = divmod(start + row, 128)
                target = tile * 256 + k // 2 * 128 + inside
                piece = tap[row : row + 64].astype(BF16)
                wp[pr, pl.ds(target, 64), pl.ds(block * chans, chans)] = piece


def turner(rows, cols):
    i = lax.broadcasted_iota(jnp.int32, (rows * cols, rows * cols), 0)
    k = lax.broadcasted_iota(jnp.int32, (rows * cols, rows * cols), 1)
    return jnp.where(k == (i % rows) * cols + i // rows, 1.0, 0.0).astype(BF16)


def picker(rows, cols, col):
    i = lax.broadcasted_iota(jnp.int32, (rows, rows * cols), 0)
    k = lax.broadcasted_iota(jnp.int32, (rows, rows * cols), 1)
    return jnp.where(k == i * cols + col, 1.0, 0.0).astype(BF16)


def fill_x(t, mine, x, rows, cols):
    chans = t.shape[1] // 2
    row = lax.broadcasted_iota(jnp.int32, (rows, 2 * chans), 0)
    for col in range(cols + 1):
        one = t[col * rows : (col + 1) * rows]
        up = jnp.where(row == 0, 0.0, pltpu.roll(one, 1, 0))
        down = jnp.where(row == rows - 1, 0.0, pltpu.roll(one, rows - 1, 0))
        for v, shifted in enumerate((up, one, down)):
            lanes = pl.ds(v * chans, chans)
            column = jnp.concatenate([shifted[:, :chans], shifted[:, chans:]], 0)
            if col < cols:
                x[pl.ds((col + 1) * 2 * rows, 2 * rows), lanes] = column.astype(BF16)
            else:
                x[pl.ds(0, 2 * rows), lanes] = jnp.where(mine == 1, column, 0.0).astype(BF16)
                x[pl.ds((cols + 1) * 2 * rows, 2 * rows), lanes] = jnp.where(mine == 0, column, 0.0).astype(BF16)


def convolve(x, wp, b_up, keep, mine, wide, done, rows, cols, copies):
    chans2 = wp.shape[2]
    chans = chans2 // 2
    column = 2 * rows
    outc = wp.shape[1] // 4
    lanes = 2 * outc
    strip_from = jnp.where(mine == 0, cols - OV, 0)
    soft = 1.0 - 0.5 / (2 * OV)
    bias = b_up[...].reshape(1, -1)
    bias = jnp.concatenate([bias, bias], -1)
    before_half = lax.broadcasted_iota(jnp.int32, (column, 128), 1) < outc % 128
    for j in range(lanes // 128):
        for pr in range(2):
            z = dot_t(x[:, pl.ds(pr * chans, chans2)], wp[pr, pl.ds(j * 256, 256), :])
            for col in range(cols):
                scale_l = scale_r = 1.0
                if col in (0, cols - OV):
                    scale_l = jnp.where(strip_from == col, soft, 1.0)
                if col in (OV - 1, cols - 1):
                    scale_r = jnp.where(strip_from + OV - 1 == col, soft, 1.0)
                here = z[(col + 1) * column : (col + 2) * column, :128] + bias[:, j * 128 : (j + 1) * 128]
                prev = z[col * column : (col + 1) * column, 128:] * scale_l
                after = z[(col + 2) * column : (col + 3) * column, 128:] * scale_r
                if (j + 1) * 128 <= outc:
                    add = prev
                elif j * 128 >= outc:
                    add = after
                else:
                    add = jnp.where(before_half, prev, after)
                tile = here + add
                for h in range(2):
                    wide[h, col * lanes // 128 + j, pl.ds(pr, rows, stride=2), :] = tile[h * rows : (h + 1) * rows]
    keep = keep[...] > 0.5
    for col in range(cols):
        shared = col < OV or col >= cols - OV
        outside = (col < strip_from) | (col >= strip_from + OV)
        for h in range(2):
            for lane in range(col * lanes, (col + 1) * lanes, 128):
                block = wide[h, lane // 128]
                if shared:
                    block = jnp.where(keep | outside, block, 0.0)
                done[h, :, pl.ds(lane, 128)] = block.astype(BF16)
        if copies and (col + 1) % (cols // LEAVES) == 0:
            copies[col // (cols // LEAVES)].start()


def leave(done, out, sems):
    width = done.shape[2] // LEAVES
    spans = [pl.ds(k * width, width) for k in range(LEAVES)]
    return [
        pltpu.make_async_copy(done.at[:, :, span], out.at[:, :, span], sems.at[k])
        for k, span in enumerate(spans)
    ]


def load_kernel(owners_hbm, own_hbm, b_time_hbm, b_up_hbm, keep, own, b_time, b_up, owners, sems):
    pairs = [(owners_hbm, owners), (own_hbm, own), (b_time_hbm, b_time), (b_up_hbm, b_up)]
    loads = [pltpu.make_async_copy(source, target, sems.at[k]) for k, (source, target) in enumerate(pairs)]
    for load in loads:
        load.start()
    mine = lax.axis_index("tile")
    loads[0].wait()
    out_row = lax.broadcasted_iota(jnp.int32, keep.shape, 0)
    owner = jnp.zeros(keep.shape, jnp.int32)
    for r in range(keep.shape[0]):
        owner = jnp.where(out_row == r, owners[r], owner)
    keep[...] = jnp.where(owner == mine, 1.0, 0.0)
    for load in loads[1:]:
        load.wait()


def pack_kernel(counts, own, own_far, latest, before):
    slots, rows, cols, chans = own.shape
    pixels = rows * cols
    mine = lax.axis_index("tile")
    two = counts[0] >= 2
    turn = turner(rows, cols)
    pick = picker(rows, cols, jnp.where(mine == 0, OV, cols - OV - 1))
    first, second = own[0].reshape(pixels, chans), own[1].reshape(pixels, chans)
    first_far, second_far = own_far[0].reshape(pixels, chans), own_far[1].reshape(pixels, chans)
    latest[pl.ds(0, pixels), :] = dot(turn, jnp.where(two, second, first)).astype(BF16)
    latest[pl.ds(pixels, rows), :] = dot(pick, jnp.where(two, second_far, first_far)).astype(BF16)
    before[pl.ds(0, pixels), :] = jnp.where(two, dot(turn, first), ABSENT).astype(BF16)
    before[pl.ds(pixels, rows), :] = jnp.where(two, dot(pick, first_far), ABSENT).astype(BF16)


def local_kernel(counts, latest, before, w_time, b_time, w_up, t0, t1, wp, lhs):
    two = counts[0] >= 2
    lhs[...] = jnp.where(two, before[...], latest[...])
    prepare_weights(w_up, wp)
    bias = b_time[...].reshape(1, -1)
    t0[...] = bias + dot(lhs[...], w_time[2])

    @pl.when(two)
    def _():
        t1[...] = bias + dot(latest[...], w_time[2]) + dot(lhs[...], w_time[1])


def add_halo(later, t, frame, weight, total):
    @pl.when(later)
    def _():
        total[...] = t[...] + dot(frame[...], weight)

    @pl.when(jnp.logical_not(later))
    def _():
        total[...] = t[...]


def near_kernel(counts, before, keep, newer, w_time, b_up, t0, t1, wp, done, t0_new, total, x, wide):
    rows = keep.shape[0] // 2
    cols = newer.shape[0] // rows - 1
    mine = lax.axis_index("tile")
    later = lax.axis_index("tm") > 0
    valid = counts[0] >= 2

    @pl.when(valid)
    def _():
        add_halo(later, t1, newer, w_time[0], total)
        fill_x(total[...], mine, x, rows, cols)
        convolve(x, wp, b_up, keep, mine, wide, done, rows, cols, [])

    @pl.when(jnp.logical_not(valid))
    def _():
        done[...] = jnp.zeros_like(done)

    add_halo(later, t0, newer, w_time[1], t0_new)


def far_kernel(
    keep, far, near_before, w_time, b_up, t0, wp, second,
    out, lhs, total, x, wide, done, sems,
):
    early = pltpu.make_async_copy(second, out.at[pl.ds(2, 2)], sems.at[LEAVES])
    early.start()
    rows = keep.shape[0] // 2
    cols = far.shape[0] // rows - 1
    mine = lax.axis_index("tile")
    place_tm = lax.axis_index("tm")
    nearer = near_before[...].astype(F32)
    further = jnp.where(place_tm >= 2, far[...].astype(F32), 0.0)
    older = jnp.where(nearer < 0.5 * ABSENT, nearer, further)
    lhs[...] = older.astype(BF16)
    add_halo(place_tm > 0, t0, lhs, w_time[0], total)
    fill_x(total[...], mine, x, rows, cols)
    copies = leave(done, out.at[pl.ds(0, 2)], sems)
    convolve(x, wp, b_up, keep, mine, wide, done, rows, cols, copies)
    for copy in copies + [early]:
        copy.wait()


def per_device(latents, frame_counts, owners, w_time, b_time, w_up, b_up):
    slots, rows, cols, chans = latents.shape
    outc = w_up.shape[3]
    ring = lax.axis_size("tm")
    pixels, extra = rows * cols, 2 * rows
    lanes = 2 * cols * outc
    shape = jax.ShapeDtypeStruct

    def step(k):
        return [(i, (i + k) % ring) for i in range(ring)]

    def stay(v):
        return pltpu.with_memory_space_constraint(v, pltpu.HBM)

    w_up = w_up.transpose(0, 1, 3, 2)
    own_far = lax.ppermute(latents, "tile", [(0, 1), (1, 0)])
    keep, own, b_time, b_up = pl.pallas_call(
        load_kernel,
        out_shape=(
            shape((extra, 128), F32),
            shape(latents.shape, BF16),
            shape(b_time.shape, F32),
            shape(b_up.shape, F32),
        ),
        in_specs=[HBM] * 4,
        out_specs=(VMEM,) * 4,
        scratch_shapes=[pltpu.SMEM(owners.shape, jnp.int32), pltpu.SemaphoreType.DMA((4,))],
        compiler_params=PARAMS,
        cost_estimate=cost(10**6, 1 << 10),
        name="load",
    )(stay(owners), stay(latents), stay(b_time), stay(b_up))
    frame = shape((pixels + rows, chans), BF16)
    latest, before = pl.pallas_call(
        pack_kernel,
        out_shape=(frame, frame),
        in_specs=[SMEM, VMEM, VMEM],
        out_specs=(VMEM,) * 2,
        compiler_params=PARAMS,
        cost_estimate=cost(3 * 10**9, 1 << 10),
        name="pack",
    )(frame_counts, own, own_far)
    newer = lax.ppermute(latest, "tm", step(1))
    far = lax.ppermute(latest, "tm", step(2))
    near_before = lax.ppermute(before, "tm", [(i, i + 1) for i in range(ring - 1)])
    partial = shape((pixels + rows, 2 * chans), F32)
    scratch = [
        pltpu.VMEM(frame.shape, BF16),
        pltpu.VMEM(partial.shape, F32),
        pltpu.VMEM(((cols + 2) * extra, 3 * chans), BF16),
        pltpu.VMEM((2, lanes // 128, extra, 128), F32),
        pltpu.VMEM((2, extra, lanes), BF16),
        pltpu.SemaphoreType.DMA((LEAVES + 1,)),
    ]
    t0, t1, wp = pl.pallas_call(
        local_kernel,
        out_shape=(
            partial,
            partial,
            shape((2, 4 * outc, 2 * chans), BF16),
        ),
        in_specs=[SMEM] + [VMEM] * 5,
        out_specs=(VMEM,) * 3,
        scratch_shapes=[pltpu.VMEM(frame.shape, BF16)],
        compiler_params=PARAMS,
        cost_estimate=cost(10**6, 1 << 10),
        name="local",
    )(frame_counts, latest, before, w_time, b_time, w_up)
    second, t0 = pl.pallas_call(
        near_kernel,
        out_shape=(shape((2, 2 * rows, lanes), BF16), partial),
        in_specs=[SMEM] + [VMEM] * 8,
        out_specs=(VMEM, VMEM),
        scratch_shapes=[pltpu.VMEM(partial.shape, F32)] + scratch[2:4],
        compiler_params=PARAMS,
        cost_estimate=cost(10**9, 4 << 20),
        name="near",
    )(frame_counts, before, keep, newer, w_time, b_up, t0, t1, wp)
    return pl.pallas_call(
        far_kernel,
        out_shape=shape((2 * slots, 2 * rows, lanes), BF16),
        in_specs=[VMEM] * 8,
        out_specs=HBM,
        scratch_shapes=scratch,
        compiler_params=PARAMS,
        cost_estimate=cost(10**9, 4 << 20),
        name="far",
    )(keep, far, near_before, w_time, b_up, t0, wp, second)


def solution(mesh):
    placed = (
        P(("videos", "tm"), None, "tile", None),
        P(("videos", "tm")),
        P("videos"),
        P(),
        P(),
        P(),
        P(),
    )
    return jax.shard_map(
        per_device,
        mesh=mesh,
        in_specs=placed,
        out_specs=P(("videos", "tm"), None, "tile"),
        check_vma=False,
    )
```

```python
import jax
import jax.numpy as jnp
from jax import lax
from jax.experimental import pallas as pl
from jax.experimental.pallas import tpu as pltpu
from jax.sharding import PartitionSpec as P

OV = 4
F32 = jnp.float32
BF16 = jnp.bfloat16
VMEM = pl.BlockSpec(memory_space=pltpu.VMEM)
SMEM = pl.BlockSpec(memory_space=pltpu.SMEM)
HBM = pl.BlockSpec(memory_space=pltpu.HBM)
LEAVES = 2
ABSENT = 16384.0
PARAMS = pltpu.CompilerParams(vmem_limit_bytes=24 << 20)


def dot(a, b):
    return jnp.dot(a, b, preferred_element_type=F32)


def dot_t(a, b):
    return lax.dot_general(a, b, (((1,), (1,)), ((), ())), preferred_element_type=F32)


def cost(flops, moved):
    return pl.CostEstimate(flops=flops, bytes_accessed=moved, transcendentals=0)


def prepare_weights(w_up, wp):
    outc, chans = w_up.shape[2], w_up.shape[3]
    for pr, block, rows in ((1, 1, (2,)), (0, 1, (1, 2)), (1, 0, (0, 1)), (0, 0, (0,))):
        taps = []
        for col in range(3):
            tap = w_up[rows[0], col].astype(F32)
            for row in rows[1:]:
                tap = tap + w_up[row, col].astype(F32)
            taps.append(tap)
        for k, tap in enumerate((taps[1] + taps[2], taps[0] + taps[1], taps[0], taps[2])):
            start = k % 2 * outc
            for row in range(0, outc, 64):
                tile, inside = divmod(start + row, 128)
                target = tile * 256 + k // 2 * 128 + inside
                piece = tap[row : row + 64].astype(BF16)
                wp[pr, pl.ds(target, 64), pl.ds(block * chans, chans)] = piece


def turner(rows, cols):
    i = lax.broadcasted_iota(jnp.int32, (rows * cols, rows * cols), 0)
    k = lax.broadcasted_iota(jnp.int32, (rows * cols, rows * cols), 1)
    return jnp.where(k == (i % rows) * cols + i // rows, 1.0, 0.0).astype(BF16)


def picker(rows, cols, col):
    i = lax.broadcasted_iota(jnp.int32, (rows, rows * cols), 0)
    k = lax.broadcasted_iota(jnp.int32, (rows, rows * cols), 1)
    return jnp.where(k == i * cols + col, 1.0, 0.0).astype(BF16)


def fill_x(t, mine, x, rows, cols):
    chans = t.shape[1] // 2
    row = lax.broadcasted_iota(jnp.int32, (rows, 2 * chans), 0)
    for col in range(cols + 1):
        one = t[col * rows : (col + 1) * rows]
        up = jnp.where(row == 0, 0.0, pltpu.roll(one, 1, 0))
        down = jnp.where(row == rows - 1, 0.0, pltpu.roll(one, rows - 1, 0))
        for v, shifted in enumerate((up, one, down)):
            lanes = pl.ds(v * chans, chans)
            column = jnp.concatenate([shifted[:, :chans], shifted[:, chans:]], 0)
            if col < cols:
                x[pl.ds((col + 1) * 2 * rows, 2 * rows), lanes] = column.astype(BF16)
            else:
                x[pl.ds(0, 2 * rows), lanes] = jnp.where(mine == 1, column, 0.0).astype(BF16)
                x[pl.ds((cols + 1) * 2 * rows, 2 * rows), lanes] = jnp.where(mine == 0, column, 0.0).astype(BF16)


def convolve(x, wp, b_up, keep, mine, wide, done, rows, cols, copies):
    chans2 = wp.shape[2]
    chans = chans2 // 2
    column = 2 * rows
    outc = wp.shape[1] // 4
    lanes = 2 * outc
    strip_from = jnp.where(mine == 0, cols - OV, 0)
    soft = 1.0 - 0.5 / (2 * OV)
    bias = b_up[...].reshape(1, -1)
    bias = jnp.concatenate([bias, bias], -1)
    before_half = lax.broadcasted_iota(jnp.int32, (column, 128), 1) < outc % 128
    for j in range(lanes // 128):
        for pr in range(2):
            z = dot_t(x[:, pl.ds(pr * chans, chans2)], wp[pr, pl.ds(j * 256, 256), :])
            for col in range(cols):
                scale_l = scale_r = 1.0
                if col in (0, cols - OV):
                    scale_l = jnp.where(strip_from == col, soft, 1.0)
                if col in (OV - 1, cols - 1):
                    scale_r = jnp.where(strip_from + OV - 1 == col, soft, 1.0)
                here = z[(col + 1) * column : (col + 2) * column, :128] + bias[:, j * 128 : (j + 1) * 128]
                prev = z[col * column : (col + 1) * column, 128:] * scale_l
                after = z[(col + 2) * column : (col + 3) * column, 128:] * scale_r
                if (j + 1) * 128 <= outc:
                    add = prev
                elif j * 128 >= outc:
                    add = after
                else:
                    add = jnp.where(before_half, prev, after)
                tile = here + add
                for h in range(2):
                    wide[h, col * lanes // 128 + j, pl.ds(pr, rows, stride=2), :] = tile[h * rows : (h + 1) * rows]
    keep = keep[...] > 0.5
    for col in range(cols):
        shared = col < OV or col >= cols - OV
        outside = (col < strip_from) | (col >= strip_from + OV)
        for h in range(2):
            for lane in range(col * lanes, (col + 1) * lanes, 128):
                block = wide[h, lane // 128]
                if shared:
                    block = jnp.where(keep | outside, block, 0.0)
                done[h, :, pl.ds(lane, 128)] = block.astype(BF16)
        if copies and (col + 1) % (cols // LEAVES) == 0:
            copies[col // (cols // LEAVES)].start()


def leave(done, out, sems):
    width = done.shape[2] // LEAVES
    spans = [pl.ds(k * width, width) for k in range(LEAVES)]
    return [
        pltpu.make_async_copy(done.at[:, :, span], out.at[:, :, span], sems.at[k])
        for k, span in enumerate(spans)
    ]


def load_kernel(owners_hbm, own_hbm, b_time_hbm, b_up_hbm, keep, own, b_time, b_up, owners, sems):
    pairs = [(owners_hbm, owners), (own_hbm, own), (b_time_hbm, b_time), (b_up_hbm, b_up)]
    loads = [pltpu.make_async_copy(source, target, sems.at[k]) for k, (source, target) in enumerate(pairs)]
    for load in loads:
        load.start()
    mine = lax.axis_index("tile")
    loads[0].wait()
    out_row = lax.broadcasted_iota(jnp.int32, keep.shape, 0)
    owner = jnp.zeros(keep.shape, jnp.int32)
    for r in range(keep.shape[0]):
        owner = jnp.where(out_row == r, owners[r], owner)
    keep[...] = jnp.where(owner == mine, 1.0, 0.0)
    for load in loads[1:]:
        load.wait()


def pack_kernel(counts, own, own_far, latest, before):
    slots, rows, cols, chans = own.shape
    pixels = rows * cols
    mine = lax.axis_index("tile")
    two = counts[0] >= 2
    turn = turner(rows, cols)
    pick = picker(rows, cols, jnp.where(mine == 0, OV, cols - OV - 1))
    first, second = own[0].reshape(pixels, chans), own[1].reshape(pixels, chans)
    first_far, second_far = own_far[0].reshape(pixels, chans), own_far[1].reshape(pixels, chans)
    latest[pl.ds(0, pixels), :] = dot(turn, jnp.where(two, second, first)).astype(BF16)
    latest[pl.ds(pixels, rows), :] = dot(pick, jnp.where(two, second_far, first_far)).astype(BF16)
    before[pl.ds(0, pixels), :] = jnp.where(two, dot(turn, first), ABSENT).astype(BF16)
    before[pl.ds(pixels, rows), :] = jnp.where(two, dot(pick, first_far), ABSENT).astype(BF16)


def local_kernel(counts, latest, before, w_time, b_time, w_up, t0, t1, wp, lhs):
    two = counts[0] >= 2
    lhs[...] = jnp.where(two, before[...], latest[...])
    prepare_weights(w_up, wp)
    bias = b_time[...].reshape(1, -1)
    t0[...] = bias + dot(lhs[...], w_time[2])

    @pl.when(two)
    def _():
        t1[...] = bias + dot(latest[...], w_time[2]) + dot(lhs[...], w_time[1])


def add_halo(later, t, frame, weight, total):
    @pl.when(later)
    def _():
        total[...] = t[...] + dot(frame[...], weight)

    @pl.when(jnp.logical_not(later))
    def _():
        total[...] = t[...]


def near_kernel(counts, before, keep, newer, w_time, b_up, t0, t1, wp, done, t0_new, total, x, wide):
    rows = keep.shape[0] // 2
    cols = newer.shape[0] // rows - 1
    mine = lax.axis_index("tile")
    later = lax.axis_index("tm") > 0
    valid = counts[0] >= 2

    @pl.when(valid)
    def _():
        add_halo(later, t1, newer, w_time[0], total)
        fill_x(total[...], mine, x, rows, cols)
        convolve(x, wp, b_up, keep, mine, wide, done, rows, cols, [])

    @pl.when(jnp.logical_not(valid))
    def _():
        done[...] = jnp.zeros_like(done)

    add_halo(later, t0, newer, w_time[1], t0_new)


def far_kernel(
    keep, far, near_before, w_time, b_up, t0, wp, second,
    out, lhs, total, x, wide, done, sems,
):
    early = pltpu.make_async_copy(second, out.at[pl.ds(2, 2)], sems.at[LEAVES])
    early.start()
    rows = keep.shape[0] // 2
    cols = far.shape[0] // rows - 1
    mine = lax.axis_index("tile")
    place_tm = lax.axis_index("tm")
    nearer = near_before[...]
    further = jnp.where(place_tm >= 2, far[...], jnp.zeros_like(far))
    older = jnp.where(nearer < jnp.asarray(0.5 * ABSENT, BF16), nearer, further)
    lhs[...] = older
    add_halo(place_tm > 0, t0, lhs, w_time[0], total)
    fill_x(total[...], mine, x, rows, cols)
    copies = leave(done, out.at[pl.ds(0, 2)], sems)
    convolve(x, wp, b_up, keep, mine, wide, done, rows, cols, copies)
    for copy in copies + [early]:
        copy.wait()


def per_device(latents, frame_counts, owners, w_time, b_time, w_up, b_up):
    slots, rows, cols, chans = latents.shape
    outc = w_up.shape[3]
    ring = lax.axis_size("tm")
    pixels, extra = rows * cols, 2 * rows
    lanes = 2 * cols * outc
    shape = jax.ShapeDtypeStruct

    def step(k):
        return [(i, (i + k) % ring) for i in range(ring)]

    def stay(v):
        return pltpu.with_memory_space_constraint(v, pltpu.HBM)

    w_up = w_up.transpose(0, 1, 3, 2)
    own_far = lax.ppermute(latents, "tile", [(0, 1), (1, 0)])
    keep, own, b_time, b_up = pl.pallas_call(
        load_kernel,
        out_shape=(
            shape((extra, 128), F32),
            shape(latents.shape, BF16),
            shape(b_time.shape, F32),
            shape(b_up.shape, F32),
        ),
        in_specs=[HBM] * 4,
        out_specs=(VMEM,) * 4,
        scratch_shapes=[pltpu.SMEM(owners.shape, jnp.int32), pltpu.SemaphoreType.DMA((4,))],
        compiler_params=PARAMS,
        cost_estimate=cost(10**6, 1 << 10),
        name="load",
    )(stay(owners), stay(latents), stay(b_time), stay(b_up))
    frame = shape((pixels + rows, chans), BF16)
    latest, before = pl.pallas_call(
        pack_kernel,
        out_shape=(frame, frame),
        in_specs=[SMEM, VMEM, VMEM],
        out_specs=(VMEM,) * 2,
        compiler_params=PARAMS,
        cost_estimate=cost(3 * 10**9, 1 << 10),
        name="pack",
    )(frame_counts, own, own_far)
    newer = lax.ppermute(latest, "tm", step(1))
    far = lax.ppermute(latest, "tm", step(2))
    near_before = lax.ppermute(before, "tm", [(i, i + 1) for i in range(ring - 1)])
    partial = shape((pixels + rows, 2 * chans), F32)
    scratch = [
        pltpu.VMEM(frame.shape, BF16),
        pltpu.VMEM(partial.shape, F32),
        pltpu.VMEM(((cols + 2) * extra, 3 * chans), BF16),
        pltpu.VMEM((2, lanes // 128, extra, 128), F32),
        pltpu.VMEM((2, extra, lanes), BF16),
        pltpu.SemaphoreType.DMA((LEAVES + 1,)),
    ]
    t0, t1, wp = pl.pallas_call(
        local_kernel,
        out_shape=(
            partial,
            partial,
            shape((2, 4 * outc, 2 * chans), BF16),
        ),
        in_specs=[SMEM] + [VMEM] * 5,
        out_specs=(VMEM,) * 3,
        scratch_shapes=[pltpu.VMEM(frame.shape, BF16)],
        compiler_params=PARAMS,
        cost_estimate=cost(10**6, 1 << 10),
        name="local",
    )(frame_counts, latest, before, w_time, b_time, w_up)
    second, t0 = pl.pallas_call(
        near_kernel,
        out_shape=(shape((2, 2 * rows, lanes), BF16), partial),
        in_specs=[SMEM] + [VMEM] * 8,
        out_specs=(VMEM, VMEM),
        scratch_shapes=[pltpu.VMEM(partial.shape, F32)] + scratch[2:4],
        compiler_params=PARAMS,
        cost_estimate=cost(10**9, 4 << 20),
        name="near",
    )(frame_counts, before, keep, newer, w_time, b_up, t0, t1, wp)
    return pl.pallas_call(
        far_kernel,
        out_shape=shape((2 * slots, 2 * rows, lanes), BF16),
        in_specs=[VMEM] * 8,
        out_specs=HBM,
        scratch_shapes=scratch,
        compiler_params=PARAMS,
        cost_estimate=cost(10**9, 4 << 20),
        name="far",
    )(keep, far, near_before, w_time, b_up, t0, wp, second)


def solution(mesh):
    placed = (
        P(("videos", "tm"), None, "tile", None),
        P(("videos", "tm")),
        P("videos"),
        P(),
        P(),
        P(),
        P(),
    )
    return jax.shard_map(
        per_device,
        mesh=mesh,
        in_specs=placed,
        out_specs=P(("videos", "tm"), None, "tile"),
        check_vma=False,
    )
```
